512 devices in a mesh: req: 64 (over x, z), tp: 8 (over y, core).
Axes of the slice: x: 4, y: 4, z: 16, core: 2. Of those that a mesh axis runs over, the one named last changes fastest.
Arguments:
- query_new: bfloat16 [8192, 2048], P('req', 'tp'), may hold values from -6 to 6
- key_new: bfloat16 [8192, 2048], P('req', 'tp'), may hold values from -6 to 6
- value_new: bfloat16 [8192, 2048], P('req', 'tp'), may hold values from -6 to 6
- mlp_hidden: bfloat16 [8192, 8192], P('req', 'tp'), may hold values from -6 to 6
- cache_pages: bfloat16 [4096, 16, 16, 256], P('req', None, 'tp'), may hold values from -6 to 6
- page_dest: int32 [4096, 1], P('req'), may hold values from 0 to 63; in each aligned block of 64 rows (0 to 63, 64 to 127, ...) at most 2 rows name the same one
- page_tag: int32 [4096], P('req'), may hold values from 0 to 3
- seg_ids: int32 [64, 128], P('req'), may hold values from 0 to 3, as said below
- attn_proj: bfloat16 [2048, 4096], P(('tp', 'req')), may hold values from -0.5 to 0.5
- mlp_down: bfloat16 [8192, 4096], P(('tp', 'req')), may hold values from -0.0625 to 0.0625
Outputs:
- layer_out: bfloat16 [8192, 4096], P('req', 'tp')
The draws below stay inside these ranges and needn't reach their ends.
Inputs may be any that keep to these rules, and one draw needn't show every extreme that they name: `seg_ids`: within each pack the ids never fall; request 0 covers exactly the first 64 tokens and requests 1 to 3 each cover one or more of the rest. `page_dest`: among the rows of one device, at most 2 pages name the same destination, a bound that some block reaches.
All inputs are finite; a program needn't handle non-finite values.
Results may differ from the reference program's by a relative error of at most 0.014.
Values may be sent and summed in bfloat16 or wider, within the bound.
A program may use at most 128 MiB of HBM per device.

```python
import math
import jax
import jax.numpy as jnp
import numpy as np
from jax import lax

D = 4096
HEADS = 16
HD = 128
ROT = 32
FF = 8192
TOK_DEV = 128
SEG_DEV = 4
PAGE_ROWS = 16
CAP = 2
PAGES_DEV = 64
SEG_MOST = 64
PACKS = 64
TOKENS = 8192
PAGES = 4096
N_REQ = 64
N_TP = 8


def draw_query_new(key, part):
    entries = jnp.clip(jax.random.normal(jax.random.fold_in(key, 1), (TOKENS, HEADS * HD), jnp.float32), -6.0, 6.0)
    return entries.astype(jnp.bfloat16)


def draw_key_new(key, part):
    entries = jnp.clip(jax.random.normal(jax.random.fold_in(key, 2), (TOKENS, HEADS * HD), jnp.float32), -6.0, 6.0)
    return entries.astype(jnp.bfloat16)


def draw_seg_ids(key, part):
    remainder = TOK_DEV - SEG_MOST
    index_row = jnp.arange(TOK_DEV, dtype=jnp.int32)

    def one_pack(pack_key):
        cut_points = jax.random.permutation(pack_key, remainder - 1)[:SEG_DEV - 2].astype(jnp.int32) + 1
        cut_points = jnp.sort(cut_points)
        later = index_row[:, None] >= (SEG_MOST + cut_points)[None, :]
        return (jnp.sum(later.astype(jnp.int32), axis=1) + (index_row >= SEG_MOST).astype(jnp.int32)).astype(jnp.int32)
    pack_keys = jax.random.split(jax.random.fold_in(key, 3), PACKS)
    return jax.vmap(one_pack)(pack_keys)


def touch_ends(array, key, least, top_value):
    longest = array.shape.index(max(array.shape))
    spots = []
    for shift in (0, 1):
        where = [jax.random.randint(jax.random.fold_in(key, axis), (), 0, length) for axis, length in enumerate(array.shape)]
        where[longest] = (where[longest] + shift) % array.shape[longest]
        spots.append(tuple(where))
    return array.at[spots[0]].set(least).at[spots[1]].set(top_value)


def levels(own_key, dims, pieces, low, top_value):
    factor_of, own = 1.0, jax.random.fold_in(own_key, 6)
    for axis_at, parts in pieces:
        heights = jnp.exp(jax.random.uniform(jax.random.fold_in(own, axis_at), (parts,), jnp.float32, low / len(pieces), top_value / len(pieces)))
        factor_of = factor_of * jnp.repeat(heights, dims[axis_at] // parts).reshape([-1 if axis == axis_at else 1 for axis in range(len(dims))])
    return factor_of


def routed_block(own_key, own, number, rows, count, top, most, skew):
    sequence = jax.random.permutation(own_key, count)
    crowded, ordinary = load_shares(count, rows * top, most, skew, True), load_shares(count, rows * top, most, skew, False)
    places = jnp.arange(count)

    def named(tallies, offset_by):
        used = int((tallies > 0).sum())
        fixed = max(1, used // 4)
        passed = fixed + (places - fixed + offset_by * (used - fixed)) % max(1, count - fixed)
        return jnp.zeros((count,), jnp.int32).at[sequence[jnp.where(places < fixed, places, passed)]].set(jnp.asarray(tallies, jnp.int32))

    tallies = jnp.where(number % 4 == 0, named(crowded, number // 4), named(ordinary, number - number // 4 - 1))
    mixed = jax.random.permutation(jax.random.fold_in(own, 3), count)
    donor, sink = mixed[0:count // 2 * 2:2], mixed[1:count // 2 * 2:2]
    room = jnp.minimum(tallies[donor] - 1, most - tallies[sink]) // 2
    room = jnp.where((donor == sequence[0]) | (sink == sequence[0]) | (tallies[sink] == 0), 0, jnp.maximum(room, 0))
    passed = jax.random.randint(jax.random.fold_in(own, 4), (count // 2,), 0, 1 << 20) % (room + 1)
    tallies = tallies.at[donor].add(-passed).at[sink].add(passed)
    labels = jnp.searchsorted(jnp.cumsum(tallies), jnp.arange(rows * top), side="right").astype(jnp.int32)
    table = labels.reshape(top, rows).T
    table = table[jax.random.permutation(jax.random.fold_in(own, 1), rows)]
    offset_by = jax.random.randint(jax.random.fold_in(own, 2), (rows, 1), 0, top)
    return jnp.take_along_axis(table, (jnp.arange(top)[None, :] + offset_by) % top, axis=1)


def load_shares(number_of, total, most, slope, full):
    loads = [(1 << 20) // math.isqrt(standing ** slope) + 1 for standing in range(1, number_of + 1)]
    largest = most if full else min(most, max(-(-total // number_of), total * loads[0] // sum(loads)))
    least = 1 if total - largest >= number_of - 1 else 0
    holding, rest = [largest] + [least] * (number_of - 1), total - largest - least * (number_of - 1)
    while rest > 0:
        candidates = [i for i in range(1, number_of) if holding[i] < largest] or [i for i in range(1, number_of) if holding[i] < most]
        mass, left = sum([loads[i] for i in candidates]), rest
        for i in candidates:
            more = min(most - holding[i], max(1, left * loads[i] // mass), rest)
            holding[i] = holding[i] + more
            rest = rest - more
    return np.array(holding)


def centred(own_key, extent, deviation, limit, shards=(), kind=jnp.bfloat16):
    array = jax.random.normal(own_key, extent, jnp.float32) * deviation
    if len(shards) > 0:
        array = levels(own_key, extent, shards, -0.22, 0.18) * array
    return jnp.clip(array, min=-limit, max=limit).astype(kind)


def setup_inputs(seed: int = 0) -> dict:
    keys = jax.random.split(jax.random.key(seed), 11)
    query_new = draw_query_new(jax.random.fold_in(keys[10], 71), 0)
    key_new = draw_key_new(jax.random.fold_in(keys[10], 71), 0)
    value_new = centred(keys[2], (TOKENS, HEADS * HD), 1.0, 6.0, ((0, 64), (1, 8)))
    mlp_hidden = centred(keys[3], (TOKENS, FF), 1.0, 6.0, ((0, 64), (1, 8)))
    cache_pages = centred(keys[4], (PAGES, PAGE_ROWS, HEADS, 2 * HD), 1.0, 6.0, ((0, 64), (2, 8)))
    page_dest_keys = jax.random.split(jax.random.fold_in(keys[5], 1), PAGES // PAGES_DEV)
    page_dest_turns = jax.random.permutation(jax.random.fold_in(keys[5], 3), PAGES // PAGES_DEV)
    page_dest = jax.vmap(lambda own, number: routed_block(jax.random.fold_in(keys[5], 2), own, number, PAGES_DEV, N_REQ, 1, CAP, 2))(page_dest_keys, page_dest_turns).reshape((PAGES, 1))
    page_tag = touch_ends(jax.random.randint(keys[6], (PAGES,), 0, SEG_DEV), jax.random.fold_in(keys[6], 1), 0, SEG_DEV - 1).astype(jnp.int32)
    seg_ids = draw_seg_ids(jax.random.fold_in(keys[10], 71), 0)
    attn_proj = centred(keys[8], (HEADS * HD, D), (HEADS * HD // 16) ** -0.5, 0.5, ((0, 512),))
    mlp_down = centred(keys[9], (FF, D), FF ** -0.5, 0.0625, ((0, 512),))
    return {"query_new": query_new, "key_new": key_new, "value_new": value_new, "mlp_hidden": mlp_hidden, "cache_pages": cache_pages, "page_dest": page_dest, "page_tag": page_tag, "seg_ids": seg_ids, "attn_proj": attn_proj, "mlp_down": mlp_down}


def rotate_heads(values, position, rot_dims):
    half_rot = rot_dims // 2
    frequency = 10000.0 ** (-2.0 * jnp.arange(half_rot, dtype=jnp.float32) / rot_dims)
    angles = position.astype(jnp.float32)[:, None] * frequency[None, :]
    cosine = jnp.cos(angles)[:, None, :]
    sine_part = jnp.sin(angles)[:, None, :]
    leading = values[..., :half_rot]
    trailing = values[..., half_rot:rot_dims]
    return jnp.concatenate([leading * cosine - trailing * sine_part, trailing * cosine + leading * sine_part, values[..., rot_dims:]], axis=-1)

def reference(query_new, key_new, value_new, mlp_hidden, cache_pages, page_dest, page_tag, seg_ids, attn_proj, mlp_down):
    slot_count = N_REQ * CAP
    destination = page_dest[:, 0]
    query_packs = query_new.reshape(PACKS, TOK_DEV, HEADS, HD)
    key_packs = key_new.reshape(PACKS, TOK_DEV, HEADS, HD)
    value_packs = value_new.reshape(PACKS, TOK_DEV, HEADS, HD)
    score_scale = 1.0 / math.sqrt(HD)
    seg_range = jnp.arange(SEG_DEV, dtype=jnp.int32)
    row_index = jnp.arange(TOK_DEV, dtype=jnp.int32)

    def one_pack(inputs):
        pack_index, query_pack, key_pack, value_pack, segment = inputs
        chosen = jnp.argsort((destination != pack_index).astype(jnp.int32), stable=True)[:slot_count].astype(jnp.int32)
        is_live = destination[chosen] == pack_index
        slot_tags = jnp.where(is_live, page_tag[chosen], -1).astype(jnp.int32)
        page_block = cache_pages[chosen].reshape(slot_count * PAGE_ROWS, HEADS, 2 * HD)
        key_tags = jnp.repeat(slot_tags, PAGE_ROWS)
        seg_first = lax.optimization_barrier(jnp.sum((segment[:, None] < seg_range[None, :]).astype(jnp.int32), axis=0))
        prefix = PAGE_ROWS * lax.optimization_barrier(jnp.sum((slot_tags[:, None] == seg_range[None, :]).astype(jnp.int32), axis=0))
        seg_match = segment[:, None] == seg_range[None, :]
        offset = lax.optimization_barrier(jnp.sum(jnp.where(seg_match, prefix[None, :] - seg_first[None, :], 0), axis=1))
        position = (row_index + offset).astype(jnp.int32)
        query_rot = rotate_heads(query_pack.astype(jnp.float32), position, ROT).astype(jnp.bfloat16)
        key_rot = rotate_heads(key_pack.astype(jnp.float32), position, ROT).astype(jnp.bfloat16)
        keys_all = jnp.concatenate([key_rot, page_block[..., :HD]], axis=0).astype(jnp.float32)
        values_all = jnp.concatenate([value_pack, page_block[..., HD:]], axis=0).astype(jnp.float32)
        scores = jnp.einsum('qhd,khd->hqk', query_rot.astype(jnp.float32), keys_all) * score_scale
        local_mask = (segment[:, None] == segment[None, :]) & (row_index[None, :] <= row_index[:, None])
        cache_mask = segment[:, None] == key_tags[None, :]
        visible = jnp.concatenate([local_mask, cache_mask], axis=1)
        scores = jnp.where(visible[None], scores, -jnp.inf)
        row_max = lax.optimization_barrier(jnp.max(scores, axis=2, keepdims=True))
        exponent = jnp.exp(scores - row_max)
        probs = (exponent / lax.optimization_barrier(jnp.sum(exponent, axis=2, keepdims=True))).astype(jnp.bfloat16)
        attention = jnp.einsum('hqk,khd->qhd', probs.astype(jnp.float32), values_all).astype(jnp.bfloat16)
        return attention.reshape(TOK_DEV, HEADS * HD)
    pack_numbers = jnp.arange(PACKS, dtype=jnp.int32)
    attention = lax.map(one_pack, (pack_numbers, query_packs, key_packs, value_packs, seg_ids)).reshape(TOKENS, HEADS * HD)
    attn_width = HEADS * HD // N_TP
    ff_width = FF // N_TP
    summed = jnp.zeros((TOKENS, D), jnp.float32)
    for group in range(N_TP):
        term = jnp.dot(attention[:, group * attn_width:(group + 1) * attn_width], attn_proj[group * attn_width:(group + 1) * attn_width], preferred_element_type=jnp.float32)
        term = term + jnp.dot(mlp_hidden[:, group * ff_width:(group + 1) * ff_width], mlp_down[group * ff_width:(group + 1) * ff_width], preferred_element_type=jnp.float32)
        rounded = lax.optimization_barrier(term.astype(jnp.bfloat16))
        summed = summed + rounded.astype(jnp.float32)
    return summed.astype(jnp.bfloat16)
```

```python
import functools
import math

import jax
import jax.numpy as jnp
from jax import lax
from jax.experimental import pallas as pl
from jax.experimental.pallas import tpu as pltpu
from jax.sharding import PartitionSpec as P

HD = 128
ROT = 32
SEG_DEV = 4
CAP = 2
NX = 4
MESH = pl.DeviceIdType.MESH


def exchange_kernel(count, w_ref, pages_ref, tags_ref, g_ref, rp_ref, rt_ref,
                    send, zr, zl, xp, xm, relay, psend, precv, tsend, trecv, local):
    me = lax.axis_index("req")
    nz = count // NX
    half_z = nz // 2
    x = me // nz
    z = me % nz
    half = w_ref.shape[1] // 2

    def at(dx, dz):
        return ((x + dx + NX) % NX) * nz + (z + dz + nz) % nz

    barrier = pltpu.get_barrier_semaphore()

    def greet(i, carry):
        pl.semaphore_signal(
            barrier, inc=1, device_id={"req": (me + i) % count}, device_id_type=MESH
        )
        return carry

    lax.fori_loop(1, count, greet, 0)
    pl.semaphore_wait(barrier, count - 1)

    def push(src, dst, recv_sem, to):
        pltpu.make_async_remote_copy(
            src_ref=src, dst_ref=dst, send_sem=send.at[0], recv_sem=recv_sem,
            device_id={"req": to}, device_id_type=MESH,
        ).start()

    def arrived(ref, sem):
        pltpu.make_async_copy(ref, ref, sem).wait()

    def page_to(to):
        pltpu.make_async_remote_copy(
            src_ref=pages_ref.at[to], dst_ref=rp_ref.at[me], send_sem=psend.at[0],
            recv_sem=precv.at[0], device_id={"req": to}, device_id_type=MESH,
        ).start()
        pltpu.make_async_remote_copy(
            src_ref=tags_ref.at[to], dst_ref=rt_ref.at[me], send_sem=tsend.at[0],
            recv_sem=trecv.at[0], device_id={"req": to}, device_id_type=MESH,
        ).start()

    def pages(dz, first):
        def one(dx, carry):
            page_to(at(dx, dz))
            return carry

        lax.fori_loop(first, NX, one, 0)

    right, left = at(0, 1), at(0, -1)
    plus, minus = at(1, 0), at(-1, 0)

    def relays(dz, slot):
        below, above = at(-1, dz), at(1, dz)
        arrived(g_ref.at[below], xp.at[slot])
        lo = g_ref.at[below, :, pl.ds(0, half)]
        push(lo, lo, relay.at[0], plus)
        arrived(g_ref.at[above], xm.at[slot])
        hi = g_ref.at[above, :, pl.ds(half, half)]
        push(hi, hi, relay.at[0], minus)

    push(w_ref, g_ref.at[me], zr.at[0], right)
    push(w_ref, g_ref.at[me], zl.at[0], left)
    push(w_ref, g_ref.at[me], xp.at[0], plus)
    push(w_ref, g_ref.at[me], xm.at[0], minus)
    own = [
        pltpu.make_async_copy(w_ref, g_ref.at[me], local.at[0]),
        pltpu.make_async_copy(pages_ref.at[me], rp_ref.at[me], precv.at[0]),
        pltpu.make_async_copy(tags_ref.at[me], rt_ref.at[me], trecv.at[0]),
    ]
    for copy in own:
        copy.start()
    pages(0, 1)
    for s in range(1, half_z + 1):
        below = g_ref.at[at(0, -s)]
        arrived(below, zr.at[s - 1])
        if s < half_z:
            push(below, below, zr.at[s], right)
        push(below, below, xp.at[2 * s - 1], plus)
        push(below, below, xm.at[2 * s - 1], minus)
        if s < half_z:
            above = g_ref.at[at(0, s)]
            arrived(above, zl.at[s - 1])
            if s < half_z - 1:
                push(above, above, zl.at[s], left)
            push(above, above, xp.at[2 * s], plus)
            push(above, above, xm.at[2 * s], minus)
        pages(s, 0)
        if s < half_z:
            pages(-s, 0)
        if s == 1:
            relays(0, 0)
        else:
            relays(-(s - 1), 2 * s - 3)
            relays(s - 1, 2 * s - 2)
    relays(-half_z, 2 * half_z - 1)
    own[0].wait()
    arrived(g_ref.at[pl.ds(0, nz)], relay.at[0])
    arrived(g_ref.at[pl.ds(0, count - 1)], send.at[0])
    arrived(rp_ref, precv.at[0])
    arrived(rt_ref, trecv.at[0])
    arrived(rp_ref.at[pl.ds(0, count - 1)], psend.at[0])
    arrived(rt_ref.at[pl.ds(0, count - 1)], tsend.at[0])


def exchange(weights, send_pages, send_tags):
    count = send_pages.shape[0]
    half_z = count // NX // 2
    any_space = pl.BlockSpec(memory_space=pl.ANY)
    dma = pltpu.SemaphoreType.DMA
    return pl.pallas_call(
        functools.partial(exchange_kernel, count),
        out_shape=(
            jax.ShapeDtypeStruct((count,) + weights.shape, weights.dtype),
            jax.ShapeDtypeStruct(send_pages.shape, send_pages.dtype),
            jax.ShapeDtypeStruct(send_tags.shape, send_tags.dtype),
        ),
        in_specs=[pl.BlockSpec(memory_space=pltpu.VMEM)] * 3,
        out_specs=(any_space, any_space, any_space),
        scratch_shapes=[
            dma((1,)), dma((half_z,)), dma((half_z,)), dma((2 * half_z,)), dma((2 * half_z,)),
            dma((1,)), dma((1,)), dma((1,)), dma((1,)), dma((1,)), dma((1,)),
        ],
        compiler_params=pltpu.CompilerParams(collective_id=0, has_side_effects=True),
        name="exchange",
    )(weights, send_pages, send_tags)


def reduce_kernel(count, part_ref, out_ref, held, send, recv):
    me = lax.axis_index("tp")
    width = out_ref.shape[1]
    barrier = pltpu.get_barrier_semaphore()
    for i in range(1, count):
        pl.semaphore_signal(
            barrier, inc=1, device_id={"tp": (me + i) % count}, device_id_type=MESH
        )
    pl.semaphore_wait(barrier, count - 1)

    def columns(g):
        return part_ref.at[:, pl.ds(pl.multiple_of(g * width, width), width)]

    copies = []
    for i in range(1, count):
        to = (me + i) % count
        copies.append(
            pltpu.make_async_remote_copy(
                src_ref=columns(to), dst_ref=held.at[i - 1], send_sem=send.at[i - 1],
                recv_sem=recv.at[i - 1], device_id={"tp": to}, device_id_type=MESH,
            )
        )
        copies[-1].start()
    total = columns(me)[...].astype(jnp.float32)
    for i, copy in enumerate(copies):
        copy.wait_recv()
        total = total + held[i].astype(jnp.float32)
    out_ref[...] = total.astype(out_ref.dtype)
    for copy in copies:
        copy.wait_send()


def reduce_groups(partial_value):
    count = lax.axis_size("tp")
    rows, columns = partial_value.shape
    width = columns // count
    return pl.pallas_call(
        functools.partial(reduce_kernel, count),
        out_shape=jax.ShapeDtypeStruct((rows, width), partial_value.dtype),
        in_specs=[pl.BlockSpec(memory_space=pltpu.VMEM)],
        out_specs=pl.BlockSpec(memory_space=pltpu.VMEM),
        scratch_shapes=[
            pltpu.VMEM((count - 1, rows, width), partial_value.dtype),
            pltpu.SemaphoreType.DMA((count - 1,)),
            pltpu.SemaphoreType.DMA((count - 1,)),
        ],
        compiler_params=pltpu.CompilerParams(collective_id=1, has_side_effects=True),
        name="reduce_groups",
    )(partial_value)


def rotate_heads(values, position, rot_dims):
    half_rot = rot_dims // 2
    frequency = 10000.0 ** (-2.0 * jnp.arange(half_rot, dtype=jnp.float32) / rot_dims)
    angles = position.astype(jnp.float32)[:, None] * frequency[None, :]
    cosine = jnp.cos(angles)[:, None, :]
    sine_part = jnp.sin(angles)[:, None, :]
    leading = values[..., :half_rot]
    trailing = values[..., half_rot:rot_dims]
    return jnp.concatenate(
        [
            leading * cosine - trailing * sine_part,
            trailing * cosine + leading * sine_part,
            values[..., rot_dims:],
        ],
        axis=-1,
    )


def masked_scores(query_rot, block_keys, segment, block_tags, score_scale):
    scores = (
        jnp.einsum("qhd,hkd->hqk", query_rot, block_keys, preferred_element_type=jnp.float32)
        * score_scale
    )
    return jnp.where((segment[:, None] == block_tags[None, :])[None], scores, -jnp.inf)


def body(
    query_new,
    key_new,
    value_new,
    mlp_hidden,
    cache_pages,
    page_dest,
    page_tag,
    seg_ids,
    attn_proj,
    mlp_down,
):
    req_count = lax.axis_size("req")
    tok_count = query_new.shape[0]
    heads_local = query_new.shape[1] // HD
    page_rows = cache_pages.shape[1]
    pages_local = cache_pages.shape[0]
    slot_count = req_count * CAP
    score_scale = 1.0 / math.sqrt(HD)
    destination = page_dest[:, 0]
    dest_match = (destination[:, None] == jnp.arange(req_count, dtype=jnp.int32)[None, :]).astype(
        jnp.int32
    )
    earlier = jnp.cumsum(dest_match, axis=0) - dest_match
    rank = jnp.sum(earlier * dest_match, axis=1)
    slot_of_page = destination * CAP + rank
    select = jnp.arange(slot_count, dtype=jnp.int32)[:, None] == slot_of_page[None, :]
    flat_pages = cache_pages.reshape(pages_local, page_rows * heads_local * 2 * HD)
    send_pages = jnp.dot(
        select.astype(jnp.bfloat16), flat_pages, preferred_element_type=jnp.float32
    ).astype(jnp.bfloat16)
    blocks = 2 * heads_local
    send_pages = (
        send_pages.reshape(req_count, CAP * page_rows, blocks, HD).transpose(0, 2, 1, 3)
    )
    send_tags = (
        jnp.sum(jnp.where(select, page_tag[None, :] + 1, 0), axis=1) - 1
    ).reshape(req_count, 1, CAP)
    send_tags = jnp.pad(send_tags, ((0, 0), (0, 0), (0, HD - CAP)))
    shard_rows, width = mlp_down.shape
    weights = jnp.concatenate([mlp_down, attn_proj.reshape(shard_rows, -1)], axis=1)
    gathered, recv_pages, recv_tags = exchange(weights, send_pages, send_tags)
    slot_tags = recv_tags[:, 0, :CAP].reshape(slot_count)
    segment = seg_ids[0]
    seg_range = jnp.arange(SEG_DEV, dtype=jnp.int32)
    seg_first = jnp.sum((segment[:, None] < seg_range[None, :]).astype(jnp.int32), axis=0)
    prefix = page_rows * jnp.sum(
        (slot_tags[:, None] == seg_range[None, :]).astype(jnp.int32), axis=0
    )
    seg_match = segment[:, None] == seg_range[None, :]
    offset = jnp.sum(jnp.where(seg_match, prefix[None, :] - seg_first[None, :], 0), axis=1)
    row_index = jnp.arange(tok_count, dtype=jnp.int32)
    position = row_index + offset
    query_rot = rotate_heads(
        query_new.reshape(tok_count, heads_local, HD).astype(jnp.float32), position, ROT
    ).astype(jnp.bfloat16)
    key_rot = rotate_heads(
        key_new.reshape(tok_count, heads_local, HD).astype(jnp.float32), position, ROT
    ).astype(jnp.bfloat16)
    value_heads = value_new.reshape(tok_count, heads_local, HD)
    local_scores = (
        jnp.einsum("qhd,khd->hqk", query_rot, key_rot, preferred_element_type=jnp.float32)
        * score_scale
    )
    causal = (segment[:, None] == segment[None, :]) & (row_index[None, :] <= row_index[:, None])
    local_scores = jnp.where(causal[None], local_scores, -jnp.inf)
    cache_rows = recv_pages.reshape(req_count, heads_local, 2, CAP * page_rows, HD)
    cache_rows = cache_rows.transpose(2, 1, 0, 3, 4).reshape(
        2, heads_local, slot_count * page_rows, HD
    )
    key_tags = jnp.repeat(slot_tags, page_rows)
    cached = masked_scores(query_rot, cache_rows[0], segment, key_tags, score_scale)
    row_max = jnp.maximum(jnp.max(local_scores, axis=2), jnp.max(cached, axis=2))
    local_exp = jnp.exp(local_scores - row_max[..., None])
    cached_exp = jnp.exp(cached - row_max[..., None])
    denominator = jnp.sum(local_exp, axis=2) + jnp.sum(cached_exp, axis=2)
    local_weights = (local_exp / denominator[..., None]).astype(jnp.bfloat16)
    cached_weights = (cached_exp / denominator[..., None]).astype(jnp.bfloat16)
    attention = jnp.einsum(
        "hqk,khd->qhd", local_weights, value_heads, preferred_element_type=jnp.float32
    )
    attention = attention + jnp.einsum(
        "hqk,hkd->qhd", cached_weights, cache_rows[1], preferred_element_type=jnp.float32
    )
    attn_flat = attention.astype(jnp.bfloat16).reshape(tok_count, heads_local * HD)
    proj_rows = attn_flat.shape[1]
    attn_part = jnp.dot(
        attn_flat,
        gathered[:, :, width:].reshape(proj_rows, width),
        preferred_element_type=jnp.float32,
    )
    partial_value = attn_part + jnp.dot(
        mlp_hidden,
        gathered[:, :, :width].reshape(req_count * shard_rows, width),
        preferred_element_type=jnp.float32,
    )
    return reduce_groups(partial_value.astype(jnp.bfloat16))


def solution(mesh):
    return jax.shard_map(
        body,
        mesh=mesh,
        in_specs=(
            P("req", "tp"),
            P("req", "tp"),
            P("req", "tp"),
            P("req", "tp"),
            P("req", None, "tp", None),
            P("req", None),
            P("req"),
            P("req", None),
            P(("tp", "req"), None),
            P(("tp", "req"), None),
        ),
        out_specs=P("req", "tp"),
        check_vma=False,
    )
```

```python
import functools
import math

import jax
import jax.numpy as jnp
from jax import lax
from jax.experimental import pallas as pl
from jax.experimental.pallas import tpu as pltpu
from jax.sharding import PartitionSpec as P

HD = 128
ROT = 32
SEG_DEV = 4
CAP = 2
NX = 4
MESH = pl.DeviceIdType.MESH


def exchange_kernel(count, w_ref, p_ref, h_ref, pages_ref, tags_ref, g_ref, ha_ref, rp_ref, rt_ref,
                    send, zr, zl, xp, xm, relay, psend, precv, tsend, trecv, wsend, wrecv,
                    hsend, hrecv):
    me = lax.axis_index("req")
    tp = lax.axis_index("tp")
    groups = ha_ref.shape[0]
    nz = count // NX
    half_z = nz // 2
    x = me // nz
    z = me % nz
    rows, proj = w_ref.shape[0], p_ref.shape[2]
    width = w_ref.shape[1] // groups

    def at(dx, dz):
        return ((x + dx + NX) % NX) * nz + (z + dz + nz) % nz

    def shard(owner, first=0, size=groups):
        return g_ref.at[pl.ds(first, size), pl.ds(pl.multiple_of(owner * rows, rows), rows), :]

    def shards(number):
        return g_ref.at[:, pl.ds(0, number * rows), :]

    barrier = pltpu.get_barrier_semaphore()

    def greet_tp(i, carry):
        pl.semaphore_signal(
            barrier, inc=1, device_id={"tp": (tp + i) % groups}, device_id_type=MESH
        )
        return carry

    def greet(i, carry):
        pl.semaphore_signal(
            barrier, inc=1, device_id={"req": (me + i) % count}, device_id_type=MESH
        )
        return carry

    lax.fori_loop(1, groups, greet_tp, 0)
    lax.fori_loop(1, count, greet, 0)
    pl.semaphore_wait(barrier, count + groups - 2)

    def push(ref, recv_sem, to):
        pltpu.make_async_remote_copy(
            src_ref=ref, dst_ref=ref, send_sem=send.at[0], recv_sem=recv_sem,
            device_id={"req": to}, device_id_type=MESH,
        ).start()

    def arrived(ref, sem):
        pltpu.make_async_copy(ref, ref, sem).wait()

    own = pl.ds(pl.multiple_of(me * rows, rows), rows)
    down_slot = g_ref.at[tp, own, pl.ds(0, width)]
    proj_slot = g_ref.at[tp, own, pl.ds(width, proj)]

    def down_of(g):
        return w_ref.at[:, pl.ds(pl.multiple_of(g * width, width), width)]

    def columns_to(i, carry):
        to = (tp + i) % groups
        for src, dst in ((down_of(to), down_slot), (p_ref.at[to], proj_slot)):
            pltpu.make_async_remote_copy(
                src_ref=src, dst_ref=dst, send_sem=wsend.at[0], recv_sem=wrecv.at[0],
                device_id={"tp": to}, device_id_type=MESH,
            ).start()
        return carry

    def hidden_to(i, carry):
        pltpu.make_async_remote_copy(
            src_ref=h_ref, dst_ref=ha_ref.at[tp], send_sem=hsend.at[0], recv_sem=hrecv.at[0],
            device_id={"tp": (tp + i) % groups}, device_id_type=MESH,
        ).start()
        return carry

    def pages(dz, first):
        def one(dx, carry):
            to = at(dx, dz)
            pltpu.make_async_remote_copy(
                src_ref=pages_ref.at[to], dst_ref=rp_ref.at[me], send_sem=psend.at[0],
                recv_sem=precv.at[0], device_id={"req": to}, device_id_type=MESH,
            ).start()
            pltpu.make_async_remote_copy(
                src_ref=tags_ref.at[to], dst_ref=rt_ref.at[me], send_sem=tsend.at[0],
                recv_sem=trecv.at[0], device_id={"req": to}, device_id_type=MESH,
            ).start()
            return carry

        lax.fori_loop(first, NX, one, 0)

    lax.fori_loop(1, groups, columns_to, 0)
    pltpu.make_async_copy(down_of(tp), down_slot, wrecv.at[0]).start()
    pltpu.make_async_copy(p_ref.at[tp], proj_slot, wrecv.at[0]).start()
    pages(0, 1)
    lax.fori_loop(1, groups, hidden_to, 0)
    pltpu.make_async_copy(h_ref, ha_ref.at[tp], hrecv.at[0]).start()
    pltpu.make_async_copy(pages_ref.at[me], rp_ref.at[me], precv.at[0]).start()
    pltpu.make_async_copy(tags_ref.at[me], rt_ref.at[me], trecv.at[0]).start()

    right, left = at(0, 1), at(0, -1)
    plus, minus = at(1, 0), at(-1, 0)

    def relays(dz, slot):
        below, above = at(-1, dz), at(1, dz)
        arrived(shard(below), xp.at[slot])
        push(shard(below, 0, groups // 2), relay.at[0], plus)
        arrived(shard(above), xm.at[slot])
        push(shard(above, groups // 2, groups // 2), relay.at[0], minus)

    mine = shard(me)
    arrived(mine, wrecv.at[0])
    push(mine, zr.at[0], right)
    push(mine, zl.at[0], left)
    push(mine, xp.at[0], plus)
    push(mine, xm.at[0], minus)
    for s in range(1, half_z + 1):
        below = shard(at(0, -s))
        arrived(below, zr.at[s - 1])
        if s < half_z:
            push(below, zr.at[s], right)
        push(below, xp.at[2 * s - 1], plus)
        push(below, xm.at[2 * s - 1], minus)
        if s < half_z:
            above = shard(at(0, s))
            arrived(above, zl.at[s - 1])
            if s < half_z - 1:
                push(above, zl.at[s], left)
            push(above, xp.at[2 * s], plus)
            push(above, xm.at[2 * s], minus)
        pages(s, 0)
        if s < half_z:
            pages(-s, 0)
        if s == 1:
            relays(0, 0)
        else:
            relays(-(s - 1), 2 * s - 3)
            relays(s - 1, 2 * s - 2)
    relays(-half_z, 2 * half_z - 1)
    arrived(shards(nz), relay.at[0])
    arrived(shards(count - 1), send.at[0])
    arrived(rp_ref, precv.at[0])
    arrived(rt_ref, trecv.at[0])
    arrived(ha_ref, hrecv.at[0])
    arrived(rp_ref.at[pl.ds(0, count - 1)], psend.at[0])
    arrived(rt_ref.at[pl.ds(0, count - 1)], tsend.at[0])
    arrived(ha_ref.at[pl.ds(0, groups - 1)], hsend.at[0])
    arrived(g_ref.at[pl.ds(0, groups - 1), pl.ds(0, rows), :], wsend.at[0])


def exchange(down, proj, hidden, send_pages, send_tags):
    count = send_pages.shape[0]
    groups = proj.shape[0]
    half_z = count // NX // 2
    any_space = pl.BlockSpec(memory_space=pl.ANY)
    dma = pltpu.SemaphoreType.DMA
    rows = down.shape[0]
    width = down.shape[1] // groups + proj.shape[2]
    return pl.pallas_call(
        functools.partial(exchange_kernel, count),
        out_shape=(
            jax.ShapeDtypeStruct((groups, count * rows, width), down.dtype),
            jax.ShapeDtypeStruct((groups,) + hidden.shape, hidden.dtype),
            jax.ShapeDtypeStruct(send_pages.shape, send_pages.dtype),
            jax.ShapeDtypeStruct(send_tags.shape, send_tags.dtype),
        ),
        in_specs=[pl.BlockSpec(memory_space=pltpu.VMEM)] * 5,
        out_specs=(any_space,) * 4,
        scratch_shapes=[
            dma((1,)), dma((half_z,)), dma((half_z,)), dma((2 * half_z,)), dma((2 * half_z,)),
        ] + [dma((1,))] * 9,
        compiler_params=pltpu.CompilerParams(collective_id=0, has_side_effects=True),
        name="exchange",
    )(down, proj, hidden, send_pages, send_tags)


def spread_kernel(groups, part_ref, out_ref, send, recv):
    me = lax.axis_index("tp")
    barrier = pltpu.get_barrier_semaphore()
    for i in range(1, groups):
        pl.semaphore_signal(
            barrier, inc=1, device_id={"tp": (me + i) % groups}, device_id_type=MESH
        )
    pl.semaphore_wait(barrier, groups - 1)
    for i in range(1, groups):
        pltpu.make_async_remote_copy(
            src_ref=part_ref, dst_ref=out_ref.at[me], send_sem=send, recv_sem=recv,
            device_id={"tp": (me + i) % groups}, device_id_type=MESH,
        ).start()
    pltpu.make_async_copy(part_ref, out_ref.at[me], recv).start()
    pltpu.make_async_copy(out_ref, out_ref, recv).wait()
    rest = out_ref.at[pl.ds(0, groups - 1)]
    pltpu.make_async_copy(rest, rest, send).wait()


def spread(part):
    groups = lax.axis_size("tp")
    return pl.pallas_call(
        functools.partial(spread_kernel, groups),
        out_shape=jax.ShapeDtypeStruct((groups,) + part.shape, part.dtype),
        in_specs=[pl.BlockSpec(memory_space=pltpu.VMEM)],
        out_specs=pl.BlockSpec(memory_space=pltpu.VMEM),
        scratch_shapes=[pltpu.SemaphoreType.DMA, pltpu.SemaphoreType.DMA],
        compiler_params=pltpu.CompilerParams(collective_id=1, has_side_effects=True),
        name="spread",
    )(part)


def project_kernel(fold, h_ref, a_ref, down_ref, proj_ref, out_ref, total, wide, flat):
    group = pl.program_id(0)
    lanes = proj_ref.shape[2]
    depth = a_ref.shape[2]
    wide[...] = proj_ref[0].astype(jnp.float32)
    for c in range(fold):
        flat[:, c * lanes:(c + 1) * lanes] = wide[pl.ds(c, depth, stride=fold), :].astype(flat.dtype)
    term = jnp.dot(h_ref[0], down_ref[0], preferred_element_type=jnp.float32)
    term = term + jnp.dot(a_ref[0], flat[...], preferred_element_type=jnp.float32)

    @pl.when(group == 0)
    def _():
        total[...] = term

    @pl.when(group > 0)
    def _():
        total[...] += term

    @pl.when(group == pl.num_programs(0) - 1)
    def _():
        out_ref[...] = total[...].astype(out_ref.dtype)


def project(hidden, attention, gathered, width):
    groups, tokens, units = hidden.shape
    depth = attention.shape[2]
    lanes = gathered.shape[2] - width
    fold = width // lanes

    def block(rows, columns, at=0):
        return pl.BlockSpec((1, rows, columns), lambda g: (g, 0, at))

    return pl.pallas_call(
        functools.partial(project_kernel, fold),
        out_shape=jax.ShapeDtypeStruct((tokens, width), hidden.dtype),
        grid=(groups,),
        in_specs=[
            block(tokens, units),
            block(tokens, depth),
            block(units, width),
            block(units, lanes, fold),
        ],
        out_specs=pl.BlockSpec((tokens, width), lambda g: (0, 0)),
        scratch_shapes=[
            pltpu.VMEM((tokens, width), jnp.float32),
            pltpu.VMEM((units, lanes), jnp.float32),
            pltpu.VMEM((depth, width), hidden.dtype),
        ],
        name="project",
    )(hidden, attention, gathered, gathered)


def rotate_heads(values, position, rot_dims):
    half_rot = rot_dims // 2
    frequency = 10000.0 ** (-2.0 * jnp.arange(half_rot, dtype=jnp.float32) / rot_dims)
    angles = position.astype(jnp.float32)[:, None] * frequency[None, :]
    cosine = jnp.cos(angles)[:, None, :]
    sine_part = jnp.sin(angles)[:, None, :]
    leading = values[..., :half_rot]
    trailing = values[..., half_rot:rot_dims]
    return jnp.concatenate(
        [
            leading * cosine - trailing * sine_part,
            trailing * cosine + leading * sine_part,
            values[..., rot_dims:],
        ],
        axis=-1,
    )


def masked_scores(query_rot, block_keys, segment, block_tags, score_scale):
    scores = (
        jnp.einsum("qhd,hkd->hqk", query_rot, block_keys, preferred_element_type=jnp.float32)
        * score_scale
    )
    return jnp.where((segment[:, None] == block_tags[None, :])[None], scores, -jnp.inf)


def body(
    query_new,
    key_new,
    value_new,
    mlp_hidden,
    cache_pages,
    page_dest,
    page_tag,
    seg_ids,
    attn_proj,
    mlp_down,
):
    req_count = lax.axis_size("req")
    tok_count = query_new.shape[0]
    heads_local = query_new.shape[1] // HD
    page_rows = cache_pages.shape[1]
    pages_local = cache_pages.shape[0]
    slot_count = req_count * CAP
    score_scale = 1.0 / math.sqrt(HD)
    destination = page_dest[:, 0]
    dest_match = (destination[:, None] == jnp.arange(req_count, dtype=jnp.int32)[None, :]).astype(
        jnp.int32
    )
    earlier = jnp.cumsum(dest_match, axis=0) - dest_match
    rank = jnp.sum(earlier * dest_match, axis=1)
    slot_of_page = destination * CAP + rank
    select = jnp.arange(slot_count, dtype=jnp.int32)[:, None] == slot_of_page[None, :]
    flat_pages = cache_pages.reshape(pages_local, page_rows * heads_local * 2 * HD)
    send_pages = jnp.dot(
        select.astype(jnp.bfloat16), flat_pages, preferred_element_type=jnp.float32
    ).astype(jnp.bfloat16)
    blocks = 2 * heads_local
    send_pages = (
        send_pages.reshape(req_count, CAP * page_rows, blocks, HD).transpose(0, 2, 1, 3)
    )
    send_tags = (
        jnp.sum(jnp.where(select, page_tag[None, :] + 1, 0), axis=1) - 1
    ).reshape(req_count, 1, CAP)
    send_tags = jnp.pad(send_tags, ((0, 0), (0, 0), (0, HD - CAP)))
    groups = lax.axis_size("tp")
    shard_rows = mlp_down.shape[0]
    proj_rows = attn_proj.shape[0]
    width = mlp_down.shape[1] // groups
    proj = attn_proj.reshape(proj_rows, groups, shard_rows // proj_rows, -1)
    proj = proj.transpose(1, 0, 2, 3).reshape(groups, shard_rows, -1)
    gathered, hidden, recv_pages, recv_tags = exchange(
        mlp_down, proj, mlp_hidden, send_pages, send_tags
    )
    slot_tags = recv_tags[:, 0, :CAP].reshape(slot_count)
    segment = seg_ids[0]
    seg_range = jnp.arange(SEG_DEV, dtype=jnp.int32)
    seg_first = jnp.sum((segment[:, None] < seg_range[None, :]).astype(jnp.int32), axis=0)
    prefix = page_rows * jnp.sum(
        (slot_tags[:, None] == seg_range[None, :]).astype(jnp.int32), axis=0
    )
    seg_match = segment[:, None] == seg_range[None, :]
    offset = jnp.sum(jnp.where(seg_match, prefix[None, :] - seg_first[None, :], 0), axis=1)
    row_index = jnp.arange(tok_count, dtype=jnp.int32)
    position = row_index + offset
    query_rot = rotate_heads(
        query_new.reshape(tok_count, heads_local, HD).astype(jnp.float32), position, ROT
    ).astype(jnp.bfloat16)
    key_rot = rotate_heads(
        key_new.reshape(tok_count, heads_local, HD).astype(jnp.float32), position, ROT
    ).astype(jnp.bfloat16)
    value_heads = value_new.reshape(tok_count, heads_local, HD)
    local_scores = (
        jnp.einsum("qhd,khd->hqk", query_rot, key_rot, preferred_element_type=jnp.float32)
        * score_scale
    )
    causal = (segment[:, None] == segment[None, :]) & (row_index[None, :] <= row_index[:, None])
    local_scores = jnp.where(causal[None], local_scores, -jnp.inf)
    cache_rows = recv_pages.reshape(req_count, heads_local, 2, CAP * page_rows, HD)
    cache_rows = cache_rows.transpose(2, 1, 0, 3, 4).reshape(
        2, heads_local, slot_count * page_rows, HD
    )
    key_tags = jnp.repeat(slot_tags, page_rows)
    cached = masked_scores(query_rot, cache_rows[0], segment, key_tags, score_scale)
    row_max = jnp.maximum(jnp.max(local_scores, axis=2), jnp.max(cached, axis=2))
    local_exp = jnp.exp(local_scores - row_max[..., None])
    cached_exp = jnp.exp(cached - row_max[..., None])
    denominator = jnp.sum(local_exp, axis=2) + jnp.sum(cached_exp, axis=2)
    local_weights = (local_exp / denominator[..., None]).astype(jnp.bfloat16)
    cached_weights = (cached_exp / denominator[..., None]).astype(jnp.bfloat16)
    attention = jnp.einsum(
        "hqk,khd->qhd", local_weights, value_heads, preferred_element_type=jnp.float32
    )
    attention = attention + jnp.einsum(
        "hqk,hkd->qhd", cached_weights, cache_rows[1], preferred_element_type=jnp.float32
    )
    attn_flat = attention.astype(jnp.bfloat16).reshape(tok_count, heads_local * HD)
    return project(hidden, spread(attn_flat), gathered, width)


def solution(mesh):
    return jax.shard_map(
        body,
        mesh=mesh,
        in_specs=(
            P("req", "tp"),
            P("req", "tp"),
            P("req", "tp"),
            P("req", "tp"),
            P("req", None, "tp", None),
            P("req", None),
            P("req"),
            P("req", None),
            P(("tp", "req"), None),
            P(("tp", "req"), None),
        ),
        out_specs=P("req", "tp"),
        check_vma=False,
    )
```

```python
import functools
import math

import jax
import jax.numpy as jnp
from jax import lax
from jax.experimental import pallas as pl
from jax.experimental.pallas import tpu as pltpu
from jax.sharding import PartitionSpec as P

HD = 128
ROT = 32
SEG_DEV = 4
CAP = 2
NX = 4
MESH = pl.DeviceIdType.MESH


def exchange_kernel(count, w_ref, p_ref, h_ref, pages_ref, tags_ref,
                    g_ref, ga_ref, ha_ref, rp_ref, rt_ref,
                    hx_ref, via_ref, vt_ref,
                    send, zr, zl, asend, arecv, psend, precv, tsend, trecv, wsend, wrecv,
                    hsend, hrecv, qsend, qrecv, vsend, vrecv, vtsend, vtrecv):
    me = lax.axis_index("req")
    tp = lax.axis_index("tp")
    groups = ha_ref.shape[0]
    nz = count // NX
    half_z = nz // 2
    x = me // nz
    z = me % nz
    rows, proj = w_ref.shape[0], p_ref.shape[2]
    width = w_ref.shape[1] // groups
    units = h_ref.shape[1] // NX

    def at(dx, dz):
        return ((x + dx + NX) % NX) * nz + (z + dz + nz) % nz

    def span(owner):
        return pl.ds(pl.multiple_of(owner * rows, rows), rows)

    def level(dz):
        return (z + dz + nz) % nz

    barrier = pltpu.get_barrier_semaphore()

    def greet_tp(i, carry):
        pl.semaphore_signal(
            barrier, inc=1, device_id={"tp": (tp + i) % groups}, device_id_type=MESH
        )
        return carry

    def greet(i, carry):
        pl.semaphore_signal(
            barrier, inc=1, device_id={"req": (me + i) % count}, device_id_type=MESH
        )
        return carry

    lax.fori_loop(1, groups, greet_tp, 0)
    lax.fori_loop(1, count, greet, 0)
    pl.semaphore_wait(barrier, count + groups - 2)

    def to_req(src, dst, send_sem, recv_sem, to):
        pltpu.make_async_remote_copy(
            src_ref=src, dst_ref=dst, send_sem=send_sem, recv_sem=recv_sem,
            device_id={"req": to}, device_id_type=MESH,
        ).start()

    def to_tp(src, dst, send_sem, recv_sem, to):
        pltpu.make_async_remote_copy(
            src_ref=src, dst_ref=dst, send_sem=send_sem, recv_sem=recv_sem,
            device_id={"tp": to}, device_id_type=MESH,
        ).start()

    def arrived(ref, sem):
        pltpu.make_async_copy(ref, ref, sem).wait()

    down_slot = g_ref.at[tp, span(z), pl.ds(0, width)]
    proj_slot = g_ref.at[tp, span(z), pl.ds(width, proj)]

    def down_of(g):
        return w_ref.at[:, pl.ds(pl.multiple_of(g * width, width), width)]

    def quarter_of(g):
        return h_ref.at[:, pl.ds(pl.multiple_of(g * units, units), units)]

    def columns_to(i, carry):
        to = (tp + i) % groups
        to_tp(down_of(to), down_slot, wsend.at[0], wrecv.at[0], to)
        to_tp(p_ref.at[to], proj_slot, wsend.at[0], wrecv.at[0], to)
        return carry

    def quarter_to(i, carry):
        to_req(quarter_of((x + i) % NX), hx_ref.at[x], qsend.at[0], qrecv.at[0], at(i, 0))
        return carry

    def hidden_to(i, carry):
        to_tp(hx_ref, ha_ref.at[tp], hsend.at[0], hrecv.at[0], (tp + i) % groups)
        return carry

    def page_to(to):
        to_req(pages_ref.at[to], rp_ref.at[me], psend.at[0], precv.at[0], to)
        to_req(tags_ref.at[to], rt_ref.at[me], tsend.at[0], trecv.at[0], to)

    def pages(dz, first, stop):
        def one(dx, carry):
            page_to(at(dx, dz))
            return carry

        lax.fori_loop(first, stop, one, 0)

    lax.fori_loop(1, groups, columns_to, 0)
    pltpu.make_async_copy(down_of(tp), down_slot, wrecv.at[0]).start()
    pltpu.make_async_copy(p_ref.at[tp], proj_slot, wrecv.at[0]).start()
    lax.fori_loop(1, NX, quarter_to, 0)
    pltpu.make_async_copy(quarter_of(x), hx_ref.at[x], qrecv.at[0]).start()

    hops = half_z // 2
    direct = NX // 2

    def by_stop(dx, carry):
        to = at(dx, -half_z)
        to_req(pages_ref.at[to], via_ref.at[dx - direct], psend.at[0], vrecv.at[0], at(0, -hops))
        to_req(tags_ref.at[to], vt_ref.at[dx - direct], tsend.at[0], vtrecv.at[0], at(0, -hops))
        return carry

    def onward(dx, carry):
        to, source = at(dx, -hops), at(0, hops)
        to_req(via_ref.at[dx - direct], rp_ref.at[source], vsend.at[0], precv.at[0], to)
        to_req(vt_ref.at[dx - direct], rt_ref.at[source], vtsend.at[0], trecv.at[0], to)
        return carry

    pages(half_z, 0, direct)
    lax.fori_loop(direct, NX, by_stop, 0)
    pltpu.make_async_copy(pages_ref.at[me], rp_ref.at[me], precv.at[0]).start()
    pltpu.make_async_copy(tags_ref.at[me], rt_ref.at[me], trecv.at[0]).start()

    right, left = at(0, 1), at(0, -1)

    def across(dz):
        src = g_ref.at[:, span(level(dz)), pl.ds(width, proj)]
        dst = ga_ref.at[:, span(at(0, dz)), :]
        pltpu.make_async_copy(src, dst, arecv.at[0]).start()

        def one(dx, carry):
            to_req(src, dst, asend.at[0], arecv.at[0], at(dx, 0))
            return carry

        lax.fori_loop(1, NX, one, 0)

    def shard(dz):
        return g_ref.at[:, span(level(dz)), :]

    arrived(shard(0), wrecv.at[0])
    to_req(shard(0), shard(0), send.at[0], zr.at[0], right)
    to_req(shard(0), shard(0), send.at[0], zl.at[0], left)
    across(0)
    arrived(hx_ref, qrecv.at[0])
    lax.fori_loop(1, groups, hidden_to, 0)
    pltpu.make_async_copy(hx_ref, ha_ref.at[tp], hrecv.at[0]).start()
    for s in range(1, half_z + 1):
        far = half_z - s
        pages(far, 0 if far else 1, NX)
        if far:
            pages(-far, 0, NX)
        if s == 2:
            arrived(via_ref, vrecv.at[0])
            arrived(vt_ref, vtrecv.at[0])
            lax.fori_loop(direct, NX, onward, 0)
        arrived(shard(-s), zr.at[s - 1])
        if s < half_z:
            to_req(shard(-s), shard(-s), send.at[0], zr.at[s], right)
            arrived(shard(s), zl.at[s - 1])
            if s < half_z - 1:
                to_req(shard(s), shard(s), send.at[0], zl.at[s], left)
            across(s)
        across(-s)
    arrived(ga_ref, arecv.at[0])
    arrived(rp_ref, precv.at[0])
    arrived(rt_ref, trecv.at[0])
    arrived(ha_ref, hrecv.at[0])
    arrived(g_ref.at[:, pl.ds(0, (nz - 1) * rows), :], send.at[0])
    arrived(ga_ref.at[:, pl.ds(0, (NX - 1) * nz * rows), :], asend.at[0])
    arrived(rp_ref.at[pl.ds(0, count - 1)], psend.at[0])
    arrived(rt_ref.at[pl.ds(0, count - 1)], tsend.at[0])
    arrived(via_ref, vsend.at[0])
    arrived(vt_ref, vtsend.at[0])
    arrived(hx_ref.at[pl.ds(0, NX - 1)], qsend.at[0])
    arrived(ha_ref.at[pl.ds(0, groups - 1)], hsend.at[0])
    arrived(g_ref.at[pl.ds(0, groups - 1), pl.ds(0, rows), :], wsend.at[0])


def exchange(down, proj, hidden, send_pages, send_tags):
    count = send_pages.shape[0]
    groups = proj.shape[0]
    nz = count // NX
    any_space = pl.BlockSpec(memory_space=pl.ANY)
    dma = pltpu.SemaphoreType.DMA
    rows, lanes = down.shape[0], proj.shape[2]
    width = down.shape[1] // groups + lanes
    packed = (NX, hidden.shape[0], hidden.shape[1] // NX)
    stops = NX - NX // 2
    return pl.pallas_call(
        functools.partial(exchange_kernel, count),
        out_shape=(
            jax.ShapeDtypeStruct((groups, nz * rows, width), down.dtype),
            jax.ShapeDtypeStruct((groups, count * rows, lanes), down.dtype),
            jax.ShapeDtypeStruct((groups,) + packed, hidden.dtype),
            jax.ShapeDtypeStruct(send_pages.shape, send_pages.dtype),
            jax.ShapeDtypeStruct(send_tags.shape, send_tags.dtype),
        ),
        in_specs=[pl.BlockSpec(memory_space=pltpu.VMEM)] * 5,
        out_specs=(any_space,) * 5,
        scratch_shapes=[
            pltpu.VMEM(packed, hidden.dtype),
            pltpu.VMEM((stops,) + send_pages.shape[1:], send_pages.dtype),
            pltpu.VMEM((stops,) + send_tags.shape[1:], send_tags.dtype),
            dma((1,)), dma((nz // 2,)), dma((nz // 2,)),
        ] + [dma((1,))] * 16,
        compiler_params=pltpu.CompilerParams(collective_id=0, has_side_effects=True),
        name="exchange",
    )(down, proj, hidden, send_pages, send_tags)


def spread_kernel(groups, count, part_ref, quarter_ref, out_ref, quarters_ref,
                  ysend, yrecv, fsend, frecv, qsend, qrecv):
    tp = lax.axis_index("tp")
    me = lax.axis_index("req")
    nz = count // NX
    x, z = me // nz, me % nz
    chips = groups // 2
    other = tp + 1 - 2 * (tp % 2)

    def along(i):
        return (tp + 2 * i) % groups

    def row(i):
        return (x + i) % NX

    barrier = pltpu.get_barrier_semaphore()
    for i in range(1, chips):
        pl.semaphore_signal(barrier, inc=1, device_id={"tp": along(i)}, device_id_type=MESH)
    pl.semaphore_signal(barrier, inc=1, device_id={"tp": other}, device_id_type=MESH)
    for i in range(1, NX):
        pl.semaphore_signal(
            barrier, inc=1, device_id={"req": row(i) * nz + z}, device_id_type=MESH
        )
    pl.semaphore_wait(barrier, chips + NX - 1)

    def copy(src, dst, send_sem, recv_sem, to):
        pltpu.make_async_remote_copy(
            src_ref=src, dst_ref=dst, send_sem=send_sem, recv_sem=recv_sem,
            device_id=to, device_id_type=MESH,
        ).start()

    def arrived(ref, sem):
        pltpu.make_async_copy(ref, ref, sem).wait()

    for i in range(1, chips):
        copy(part_ref, out_ref.at[tp], ysend.at[0], yrecv.at[i - 1], {"tp": along(i)})
    copy(part_ref, out_ref.at[tp], fsend.at[0], frecv.at[0], {"tp": other})
    for i in range(1, NX):
        copy(quarter_ref.at[row(i)], quarters_ref.at[x], qsend.at[0], qrecv.at[0],
             {"req": row(i) * nz + z})
    own = pltpu.make_async_copy(part_ref, out_ref.at[tp], yrecv.at[chips - 1])
    own.start()
    pltpu.make_async_copy(quarter_ref.at[x], quarters_ref.at[x], qrecv.at[0]).start()
    for i in (1, 3, 2):
        block = out_ref.at[along(chips - i)]
        arrived(block, yrecv.at[i - 1])
        copy(block, block, fsend.at[0], frecv.at[0], {"tp": other})
    own.wait()
    arrived(out_ref.at[pl.ds(0, chips)], frecv.at[0])
    arrived(quarters_ref, qrecv.at[0])
    arrived(out_ref.at[pl.ds(0, chips - 1)], ysend.at[0])
    arrived(out_ref.at[pl.ds(0, chips)], fsend.at[0])
    arrived(quarters_ref.at[pl.ds(0, NX - 1)], qsend.at[0])


def spread(part, quarters):
    groups = lax.axis_size("tp")
    vmem = pl.BlockSpec(memory_space=pltpu.VMEM)
    dma = pltpu.SemaphoreType.DMA
    return pl.pallas_call(
        functools.partial(spread_kernel, groups, lax.axis_size("req")),
        out_shape=(
            jax.ShapeDtypeStruct((groups,) + part.shape, part.dtype),
            jax.ShapeDtypeStruct(quarters.shape, quarters.dtype),
        ),
        in_specs=[vmem, vmem],
        out_specs=(vmem, vmem),
        scratch_shapes=[
            dma((1,)), dma((groups // 2,)), dma((1,)), dma((1,)), dma((1,)), dma((1,)),
        ],
        compiler_params=pltpu.CompilerParams(collective_id=1, has_side_effects=True),
        name="spread",
    )(part, quarters)


def down_kernel(h_ref, down_ref, out_ref, total):
    group = pl.program_id(0)
    packs, tokens, units = h_ref.shape[1:]
    hidden = h_ref[0].reshape(packs * tokens, units)
    term = jnp.dot(hidden, down_ref[0], preferred_element_type=jnp.float32)

    @pl.when(group == 0)
    def _():
        total[...] = term

    @pl.when(group > 0)
    def _():
        total[...] += term

    @pl.when(group == pl.num_programs(0) - 1)
    def _():
        out_ref[...] = total[...].reshape(out_ref.shape).astype(out_ref.dtype)


def down_quarters(hidden, gathered, width):
    groups, packs, tokens, units = hidden.shape
    return pl.pallas_call(
        down_kernel,
        out_shape=jax.ShapeDtypeStruct((packs, tokens, width), hidden.dtype),
        grid=(groups,),
        in_specs=[
            pl.BlockSpec((1, packs, tokens, units), lambda g: (g, 0, 0, 0)),
            pl.BlockSpec((1, units, width), lambda g: (g, 0, 0)),
        ],
        out_specs=pl.BlockSpec((packs, tokens, width), lambda g: (0, 0, 0)),
        scratch_shapes=[pltpu.VMEM((packs * tokens, width), jnp.float32)],
        name="down_quarters",
    )(hidden, gathered)


def project_kernel(fold, a_ref, quarters_ref, proj_ref, out_ref, total, wide, flat):
    group = pl.program_id(0)
    lanes = proj_ref.shape[2]
    depth = a_ref.shape[2]
    wide[...] = proj_ref[0].astype(jnp.float32)
    for c in range(fold):
        flat[:, c * lanes:(c + 1) * lanes] = wide[pl.ds(c, depth, stride=fold), :].astype(flat.dtype)
    term = jnp.dot(a_ref[0], flat[...], preferred_element_type=jnp.float32)

    @pl.when(group == 0)
    def _():
        total[...] = term + jnp.sum(quarters_ref[...].astype(jnp.float32), axis=0)

    @pl.when(group > 0)
    def _():
        total[...] += term

    @pl.when(group == pl.num_programs(0) - 1)
    def _():
        out_ref[...] = total[...].astype(out_ref.dtype)


def project(attention, quarters, proj):
    groups, tokens, depth = attention.shape
    width = quarters.shape[2]
    units, lanes = proj.shape[1:]
    return pl.pallas_call(
        functools.partial(project_kernel, width // lanes),
        out_shape=jax.ShapeDtypeStruct((tokens, width), attention.dtype),
        grid=(groups,),
        in_specs=[
            pl.BlockSpec((1, tokens, depth), lambda g: (g, 0, 0)),
            pl.BlockSpec(quarters.shape, lambda g: (0, 0, 0)),
            pl.BlockSpec((1, units, lanes), lambda g: (g, 0, 0)),
        ],
        out_specs=pl.BlockSpec((tokens, width), lambda g: (0, 0)),
        scratch_shapes=[
            pltpu.VMEM((tokens, width), jnp.float32),
            pltpu.VMEM((units, lanes), jnp.float32),
            pltpu.VMEM((depth, width), attention.dtype),
        ],
        name="project",
    )(attention, quarters, proj)


def rotate_heads(values, position, rot_dims):
    half_rot = rot_dims // 2
    frequency = 10000.0 ** (-2.0 * jnp.arange(half_rot, dtype=jnp.float32) / rot_dims)
    angles = position.astype(jnp.float32)[:, None] * frequency[None, :]
    cosine = jnp.cos(angles)[:, None, :]
    sine_part = jnp.sin(angles)[:, None, :]
    leading = values[..., :half_rot]
    trailing = values[..., half_rot:rot_dims]
    return jnp.concatenate(
        [
            leading * cosine - trailing * sine_part,
            trailing * cosine + leading * sine_part,
            values[..., rot_dims:],
        ],
        axis=-1,
    )


def masked_scores(query_rot, block_keys, segment, block_tags, score_scale):
    scores = (
        jnp.einsum("qhd,hkd->hqk", query_rot, block_keys, preferred_element_type=jnp.float32)
        * score_scale
    )
    return jnp.where((segment[:, None] == block_tags[None, :])[None], scores, -jnp.inf)


def body(
    query_new,
    key_new,
    value_new,
    mlp_hidden,
    cache_pages,
    page_dest,
    page_tag,
    seg_ids,
    attn_proj,
    mlp_down,
):
    req_count = lax.axis_size("req")
    tok_count = query_new.shape[0]
    heads_local = query_new.shape[1] // HD
    page_rows = cache_pages.shape[1]
    pages_local = cache_pages.shape[0]
    slot_count = req_count * CAP
    score_scale = 1.0 / math.sqrt(HD)
    destination = page_dest[:, 0]
    dest_match = (destination[:, None] == jnp.arange(req_count, dtype=jnp.int32)[None, :]).astype(
        jnp.int32
    )
    earlier = jnp.cumsum(dest_match, axis=0) - dest_match
    rank = jnp.sum(earlier * dest_match, axis=1)
    slot_of_page = destination * CAP + rank
    select = jnp.arange(slot_count, dtype=jnp.int32)[:, None] == slot_of_page[None, :]
    flat_pages = cache_pages.reshape(pages_local, page_rows * heads_local * 2 * HD)
    send_pages = jnp.dot(
        select.astype(jnp.bfloat16), flat_pages, preferred_element_type=jnp.float32
    ).astype(jnp.bfloat16)
    blocks = 2 * heads_local
    send_pages = (
        send_pages.reshape(req_count, CAP * page_rows, blocks, HD).transpose(0, 2, 1, 3)
    )
    send_tags = (
        jnp.sum(jnp.where(select, page_tag[None, :] + 1, 0), axis=1) - 1
    ).reshape(req_count, 1, CAP)
    send_tags = jnp.pad(send_tags, ((0, 0), (0, 0), (0, HD - CAP)))
    groups = lax.axis_size("tp")
    shard_rows = mlp_down.shape[0]
    proj_rows = attn_proj.shape[0]
    width = mlp_down.shape[1] // groups
    proj = attn_proj.reshape(proj_rows, groups, shard_rows // proj_rows, -1)
    proj = proj.transpose(1, 0, 2, 3).reshape(groups, shard_rows, -1)
    gathered, proj_all, hidden, recv_pages, recv_tags = exchange(
        mlp_down, proj, mlp_hidden, send_pages, send_tags
    )
    slot_tags = recv_tags[:, 0, :CAP].reshape(slot_count)
    segment = seg_ids[0]
    seg_range = jnp.arange(SEG_DEV, dtype=jnp.int32)
    seg_first = jnp.sum((segment[:, None] < seg_range[None, :]).astype(jnp.int32), axis=0)
    prefix = page_rows * jnp.sum(
        (slot_tags[:, None] == seg_range[None, :]).astype(jnp.int32), axis=0
    )
    seg_match = segment[:, None] == seg_range[None, :]
    offset = jnp.sum(jnp.where(seg_match, prefix[None, :] - seg_first[None, :], 0), axis=1)
    row_index = jnp.arange(tok_count, dtype=jnp.int32)
    position = row_index + offset
    query_rot = rotate_heads(
        query_new.reshape(tok_count, heads_local, HD).astype(jnp.float32), position, ROT
    ).astype(jnp.bfloat16)
    key_rot = rotate_heads(
        key_new.reshape(tok_count, heads_local, HD).astype(jnp.float32), position, ROT
    ).astype(jnp.bfloat16)
    value_heads = value_new.reshape(tok_count, heads_local, HD)
    local_scores = (
        jnp.einsum("qhd,khd->hqk", query_rot, key_rot, preferred_element_type=jnp.float32)
        * score_scale
    )
    causal = (segment[:, None] == segment[None, :]) & (row_index[None, :] <= row_index[:, None])
    local_scores = jnp.where(causal[None], local_scores, -jnp.inf)
    cache_rows = recv_pages.reshape(req_count, heads_local, 2, CAP * page_rows, HD)
    cache_rows = cache_rows.transpose(2, 1, 0, 3, 4).reshape(
        2, heads_local, slot_count * page_rows, HD
    )
    key_tags = jnp.repeat(slot_tags, page_rows)
    cached = masked_scores(query_rot, cache_rows[0], segment, key_tags, score_scale)
    row_max = jnp.maximum(jnp.max(local_scores, axis=2), jnp.max(cached, axis=2))
    local_exp = jnp.exp(local_scores - row_max[..., None])
    cached_exp = jnp.exp(cached - row_max[..., None])
    denominator = jnp.sum(local_exp, axis=2) + jnp.sum(cached_exp, axis=2)
    local_weights = (local_exp / denominator[..., None]).astype(jnp.bfloat16)
    cached_weights = (cached_exp / denominator[..., None]).astype(jnp.bfloat16)
    attention = jnp.einsum(
        "hqk,khd->qhd", local_weights, value_heads, preferred_element_type=jnp.float32
    )
    attention = attention + jnp.einsum(
        "hqk,hkd->qhd", cached_weights, cache_rows[1], preferred_element_type=jnp.float32
    )
    attn_flat = attention.astype(jnp.bfloat16).reshape(tok_count, heads_local * HD)
    attention_all, quarters = spread(attn_flat, down_quarters(hidden, gathered, width))
    return project(attention_all, quarters, proj_all)


def solution(mesh):
    return jax.shard_map(
        body,
        mesh=mesh,
        in_specs=(
            P("req", "tp"),
            P("req", "tp"),
            P("req", "tp"),
            P("req", "tp"),
            P("req", None, "tp", None),
            P("req", None),
            P("req"),
            P("req", None),
            P(("tp", "req"), None),
            P(("tp", "req"), None),
        ),
        out_specs=P("req", "tp"),
        check_vma=False,
    )
```

```python
import functools
import math

import jax
import jax.numpy as jnp
from jax import lax
from jax.experimental import pallas as pl
from jax.experimental.pallas import tpu as pltpu
from jax.sharding import PartitionSpec as P

HD = 128
ROT = 32
SEG_DEV = 4
CAP = 2
NX = 4
MESH = pl.DeviceIdType.MESH


def exchange_kernel(count, w_ref, p_ref, h_ref, pages_ref, tags_ref, g_ref, ha_ref, rp_ref, rt_ref,
                    via_ref, vt_ref, send, zr, zl, xp, xm, relay, psend, precv, tsend, trecv, wsend, wrecv,
                    hsend, hrecv, vsend, vrecv, vtsend, vtrecv):
    me = lax.axis_index("req")
    tp = lax.axis_index("tp")
    groups = ha_ref.shape[0]
    nz = count // NX
    half_z = nz // 2
    x = me // nz
    z = me % nz
    rows, proj = w_ref.shape[0], p_ref.shape[2]
    width = w_ref.shape[1] // groups

    def at(dx, dz):
        return ((x + dx + NX) % NX) * nz + (z + dz + nz) % nz

    def shard(owner, first=0, size=groups):
        return g_ref.at[pl.ds(first, size), pl.ds(pl.multiple_of(owner * rows, rows), rows), :]

    def shards(number):
        return g_ref.at[:, pl.ds(0, number * rows), :]

    barrier = pltpu.get_barrier_semaphore()

    def greet_tp(i, carry):
        pl.semaphore_signal(
            barrier, inc=1, device_id={"tp": (tp + i) % groups}, device_id_type=MESH
        )
        return carry

    def greet(i, carry):
        pl.semaphore_signal(
            barrier, inc=1, device_id={"req": (me + i) % count}, device_id_type=MESH
        )
        return carry

    lax.fori_loop(1, groups, greet_tp, 0)
    lax.fori_loop(1, count, greet, 0)
    pl.semaphore_wait(barrier, count + groups - 2)

    def push(ref, recv_sem, to):
        pltpu.make_async_remote_copy(
            src_ref=ref, dst_ref=ref, send_sem=send.at[0], recv_sem=recv_sem,
            device_id={"req": to}, device_id_type=MESH,
        ).start()

    def arrived(ref, sem):
        pltpu.make_async_copy(ref, ref, sem).wait()

    own = pl.ds(pl.multiple_of(me * rows, rows), rows)
    down_slot = g_ref.at[tp, own, pl.ds(0, width)]
    proj_slot = g_ref.at[tp, own, pl.ds(width, proj)]

    def down_of(g):
        return w_ref.at[:, pl.ds(pl.multiple_of(g * width, width), width)]

    def columns_to(i, carry):
        to = (tp + i) % groups
        for src, dst in ((down_of(to), down_slot), (p_ref.at[to], proj_slot)):
            pltpu.make_async_remote_copy(
                src_ref=src, dst_ref=dst, send_sem=wsend.at[0], recv_sem=wrecv.at[0],
                device_id={"tp": to}, device_id_type=MESH,
            ).start()
        return carry

    def hidden_to(i, carry):
        pltpu.make_async_remote_copy(
            src_ref=h_ref, dst_ref=ha_ref.at[tp], send_sem=hsend.at[0], recv_sem=hrecv.at[0],
            device_id={"tp": (tp + i) % groups}, device_id_type=MESH,
        ).start()
        return carry

    def to_req(src, dst, send_sem, recv_sem, to):
        pltpu.make_async_remote_copy(
            src_ref=src, dst_ref=dst, send_sem=send_sem, recv_sem=recv_sem,
            device_id={"req": to}, device_id_type=MESH,
        ).start()

    def pages(dz, first, stop=NX):
        def one(dx, carry):
            to = at(dx, dz)
            to_req(pages_ref.at[to], rp_ref.at[me], psend.at[0], precv.at[0], to)
            to_req(tags_ref.at[to], rt_ref.at[me], tsend.at[0], trecv.at[0], to)
            return carry

        lax.fori_loop(first, stop, one, 0)

    hops = half_z // 2
    direct = NX // 2

    def by_stop(dx, carry):
        to = at(dx, -half_z)
        to_req(pages_ref.at[to], via_ref.at[dx - direct], psend.at[0], vrecv.at[0], at(0, -hops))
        to_req(tags_ref.at[to], vt_ref.at[dx - direct], tsend.at[0], vtrecv.at[0], at(0, -hops))
        return carry

    def onward(dx, carry):
        to, source = at(dx, -hops), at(0, hops)
        to_req(via_ref.at[dx - direct], rp_ref.at[source], vsend.at[0], precv.at[0], to)
        to_req(vt_ref.at[dx - direct], rt_ref.at[source], vtsend.at[0], trecv.at[0], to)
        return carry

    lax.fori_loop(1, groups, columns_to, 0)
    pltpu.make_async_copy(down_of(tp), down_slot, wrecv.at[0]).start()
    pltpu.make_async_copy(p_ref.at[tp], proj_slot, wrecv.at[0]).start()
    pages(0, 1)
    lax.fori_loop(direct, NX, by_stop, 0)
    lax.fori_loop(1, groups, hidden_to, 0)
    pltpu.make_async_copy(h_ref, ha_ref.at[tp], hrecv.at[0]).start()
    pltpu.make_async_copy(pages_ref.at[me], rp_ref.at[me], precv.at[0]).start()
    pltpu.make_async_copy(tags_ref.at[me], rt_ref.at[me], trecv.at[0]).start()

    right, left = at(0, 1), at(0, -1)
    plus, minus = at(1, 0), at(-1, 0)

    def relays(dz, slot):
        below, above = at(-1, dz), at(1, dz)
        arrived(shard(below), xp.at[slot])
        push(shard(below, 0, groups // 2), relay.at[0], plus)
        arrived(shard(above), xm.at[slot])
        push(shard(above, groups // 2, groups // 2), relay.at[0], minus)

    mine = shard(me)
    arrived(mine, wrecv.at[0])
    push(mine, zr.at[0], right)
    push(mine, zl.at[0], left)
    push(mine, xp.at[0], plus)
    push(mine, xm.at[0], minus)
    for s in range(1, half_z + 1):
        below = shard(at(0, -s))
        arrived(below, zr.at[s - 1])
        if s < half_z:
            push(below, zr.at[s], right)
        push(below, xp.at[2 * s - 1], plus)
        push(below, xm.at[2 * s - 1], minus)
        if s < half_z:
            above = shard(at(0, s))
            arrived(above, zl.at[s - 1])
            if s < half_z - 1:
                push(above, zl.at[s], left)
            push(above, xp.at[2 * s], plus)
            push(above, xm.at[2 * s], minus)
        pages(s, 0, NX if s < half_z else direct)
        if s < half_z:
            pages(-s, 0)
        if s == 2:
            arrived(via_ref, vrecv.at[0])
            arrived(vt_ref, vtrecv.at[0])
            lax.fori_loop(direct, NX, onward, 0)
        if s == 1:
            relays(0, 0)
        else:
            relays(-(s - 1), 2 * s - 3)
            relays(s - 1, 2 * s - 2)
    relays(-half_z, 2 * half_z - 1)
    arrived(shards(nz), relay.at[0])
    arrived(shards(count - 1), send.at[0])
    arrived(rp_ref, precv.at[0])
    arrived(rt_ref, trecv.at[0])
    arrived(ha_ref, hrecv.at[0])
    arrived(rp_ref.at[pl.ds(0, count - 1)], psend.at[0])
    arrived(rt_ref.at[pl.ds(0, count - 1)], tsend.at[0])
    arrived(via_ref, vsend.at[0])
    arrived(vt_ref, vtsend.at[0])
    arrived(ha_ref.at[pl.ds(0, groups - 1)], hsend.at[0])
    arrived(g_ref.at[pl.ds(0, groups - 1), pl.ds(0, rows), :], wsend.at[0])


def exchange(down, proj, hidden, send_pages, send_tags):
    count = send_pages.shape[0]
    groups = proj.shape[0]
    half_z = count // NX // 2
    any_space = pl.BlockSpec(memory_space=pl.ANY)
    dma = pltpu.SemaphoreType.DMA
    rows = down.shape[0]
    width = down.shape[1] // groups + proj.shape[2]
    return pl.pallas_call(
        functools.partial(exchange_kernel, count),
        out_shape=(
            jax.ShapeDtypeStruct((groups, count * rows, width), down.dtype),
            jax.ShapeDtypeStruct((groups,) + hidden.shape, hidden.dtype),
            jax.ShapeDtypeStruct(send_pages.shape, send_pages.dtype),
            jax.ShapeDtypeStruct(send_tags.shape, send_tags.dtype),
        ),
        in_specs=[pl.BlockSpec(memory_space=pltpu.VMEM)] * 5,
        out_specs=(any_space,) * 4,
        scratch_shapes=[
            pltpu.VMEM((NX - NX // 2,) + send_pages.shape[1:], send_pages.dtype),
            pltpu.VMEM((NX - NX // 2,) + send_tags.shape[1:], send_tags.dtype),
            dma((1,)), dma((half_z,)), dma((half_z,)), dma((2 * half_z,)), dma((2 * half_z,)),
        ] + [dma((1,))] * 13,
        compiler_params=pltpu.CompilerParams(collective_id=0, has_side_effects=True),
        name="exchange",
    )(down, proj, hidden, send_pages, send_tags)


def project_kernel(groups, part_ref, h_ref, g_ref, out_ref,
                   all_ref, hid, wts, total, wide, flat, send, recv, hsem, gsem):
    me = lax.axis_index("tp")
    width = out_ref.shape[1]
    lanes = g_ref.shape[2] - width
    depth = part_ref.shape[1]

    def load(g, carry):
        pltpu.make_async_copy(h_ref.at[g], hid.at[g], hsem.at[g]).start()
        pltpu.make_async_copy(g_ref.at[g], wts.at[g], gsem.at[g]).start()
        return carry

    barrier = pltpu.get_barrier_semaphore()
    for i in range(1, groups):
        pl.semaphore_signal(
            barrier, inc=1, device_id={"tp": (me + i) % groups}, device_id_type=MESH
        )
    lax.fori_loop(0, groups, load, 0)
    pl.semaphore_wait(barrier, groups - 1)
    for i in range(1, groups):
        pltpu.make_async_remote_copy(
            src_ref=part_ref, dst_ref=all_ref.at[me], send_sem=send.at[0], recv_sem=recv.at[0],
            device_id={"tp": (me + i) % groups}, device_id_type=MESH,
        ).start()
    pltpu.make_async_copy(part_ref, all_ref.at[me], recv.at[0]).start()
    total[...] = jnp.zeros_like(total)

    def local_term(g, carry):
        pltpu.make_async_copy(h_ref.at[g], hid.at[g], hsem.at[g]).wait()
        pltpu.make_async_copy(g_ref.at[g], wts.at[g], gsem.at[g]).wait()
        total[...] += jnp.dot(hid[g], wts[g, :, :width], preferred_element_type=jnp.float32)
        wide[...] = wts[g, :, width:].astype(jnp.float32)
        for c in range(width // lanes):
            flat[g, :, c * lanes:(c + 1) * lanes] = wide[
                pl.ds(c, depth, stride=width // lanes), :
            ].astype(flat.dtype)
        return carry

    lax.fori_loop(0, groups, local_term, 0)
    pltpu.make_async_copy(all_ref, all_ref, recv.at[0]).wait()

    def spread_term(g, carry):
        total[...] += jnp.dot(all_ref[g], flat[g], preferred_element_type=jnp.float32)
        return carry

    lax.fori_loop(0, groups, spread_term, 0)
    out_ref[...] = total[...].astype(out_ref.dtype)
    rest = all_ref.at[pl.ds(0, groups - 1)]
    pltpu.make_async_copy(rest, rest, send.at[0]).wait()


def project(part, hidden, gathered, width):
    groups, units = gathered.shape[:2]
    tokens, depth = part.shape
    lanes = gathered.shape[2] - width
    vmem = pl.BlockSpec(memory_space=pltpu.VMEM)
    any_space = pl.BlockSpec(memory_space=pl.ANY)
    dma = pltpu.SemaphoreType.DMA
    return pl.pallas_call(
        functools.partial(project_kernel, groups),
        out_shape=jax.ShapeDtypeStruct((tokens, width), part.dtype),
        in_specs=[vmem, any_space, any_space],
        out_specs=vmem,
        scratch_shapes=[
            pltpu.VMEM((groups,) + part.shape, part.dtype),
            pltpu.VMEM(hidden.shape, hidden.dtype),
            pltpu.VMEM(gathered.shape, gathered.dtype),
            pltpu.VMEM((tokens, width), jnp.float32),
            pltpu.VMEM((units, lanes), jnp.float32),
            pltpu.VMEM((groups, depth, width), part.dtype),
            dma((1,)), dma((1,)), dma((groups,)), dma((groups,)),
        ],
        compiler_params=pltpu.CompilerParams(collective_id=1, has_side_effects=True),
        name="project",
    )(part, hidden, gathered)


def rotate_heads(values, position, rot_dims):
    half_rot = rot_dims // 2
    frequency = 10000.0 ** (-2.0 * jnp.arange(half_rot, dtype=jnp.float32) / rot_dims)
    angles = position.astype(jnp.float32)[:, None] * frequency[None, :]
    cosine = jnp.cos(angles)[:, None, :]
    sine_part = jnp.sin(angles)[:, None, :]
    leading = values[..., :half_rot]
    trailing = values[..., half_rot:rot_dims]
    return jnp.concatenate(
        [
            leading * cosine - trailing * sine_part,
            trailing * cosine + leading * sine_part,
            values[..., rot_dims:],
        ],
        axis=-1,
    )


def masked_scores(query_rot, block_keys, segment, block_tags, score_scale):
    scores = (
        jnp.einsum("qhd,hkd->hqk", query_rot, block_keys, preferred_element_type=jnp.float32)
        * score_scale
    )
    return jnp.where((segment[:, None] == block_tags[None, :])[None], scores, -jnp.inf)


def body(
    query_new,
    key_new,
    value_new,
    mlp_hidden,
    cache_pages,
    page_dest,
    page_tag,
    seg_ids,
    attn_proj,
    mlp_down,
):
    req_count = lax.axis_size("req")
    tok_count = query_new.shape[0]
    heads_local = query_new.shape[1] // HD
    page_rows = cache_pages.shape[1]
    pages_local = cache_pages.shape[0]
    slot_count = req_count * CAP
    score_scale = 1.0 / math.sqrt(HD)
    destination = page_dest[:, 0]
    dest_match = (destination[:, None] == jnp.arange(req_count, dtype=jnp.int32)[None, :]).astype(
        jnp.int32
    )
    earlier = jnp.cumsum(dest_match, axis=0) - dest_match
    rank = jnp.sum(earlier * dest_match, axis=1)
    slot_of_page = destination * CAP + rank
    select = jnp.arange(slot_count, dtype=jnp.int32)[:, None] == slot_of_page[None, :]
    flat_pages = cache_pages.reshape(pages_local, page_rows * heads_local * 2 * HD)
    send_pages = jnp.dot(
        select.astype(jnp.bfloat16), flat_pages, preferred_element_type=jnp.float32
    ).astype(jnp.bfloat16)
    blocks = 2 * heads_local
    send_pages = (
        send_pages.reshape(req_count, CAP * page_rows, blocks, HD).transpose(0, 2, 1, 3)
    )
    send_tags = (
        jnp.sum(jnp.where(select, page_tag[None, :] + 1, 0), axis=1) - 1
    ).reshape(req_count, 1, CAP)
    send_tags = jnp.pad(send_tags, ((0, 0), (0, 0), (0, HD - CAP)))
    groups = lax.axis_size("tp")
    shard_rows = mlp_down.shape[0]
    proj_rows = attn_proj.shape[0]
    width = mlp_down.shape[1] // groups
    proj = attn_proj.reshape(proj_rows, groups, shard_rows // proj_rows, -1)
    proj = proj.transpose(1, 0, 2, 3).reshape(groups, shard_rows, -1)
    gathered, hidden, recv_pages, recv_tags = exchange(
        mlp_down, proj, mlp_hidden, send_pages, send_tags
    )
    slot_tags = recv_tags[:, 0, :CAP].reshape(slot_count)
    segment = seg_ids[0]
    seg_range = jnp.arange(SEG_DEV, dtype=jnp.int32)
    seg_first = jnp.sum((segment[:, None] < seg_range[None, :]).astype(jnp.int32), axis=0)
    prefix = page_rows * jnp.sum(
        (slot_tags[:, None] == seg_range[None, :]).astype(jnp.int32), axis=0
    )
    seg_match = segment[:, None] == seg_range[None, :]
    offset = jnp.sum(jnp.where(seg_match, prefix[None, :] - seg_first[None, :], 0), axis=1)
    row_index = jnp.arange(tok_count, dtype=jnp.int32)
    position = row_index + offset
    query_rot = rotate_heads(
        query_new.reshape(tok_count, heads_local, HD).astype(jnp.float32), position, ROT
    ).astype(jnp.bfloat16)
    key_rot = rotate_heads(
        key_new.reshape(tok_count, heads_local, HD).astype(jnp.float32), position, ROT
    ).astype(jnp.bfloat16)
    value_heads = value_new.reshape(tok_count, heads_local, HD)
    local_scores = (
        jnp.einsum("qhd,khd->hqk", query_rot, key_rot, preferred_element_type=jnp.float32)
        * score_scale
    )
    causal = (segment[:, None] == segment[None, :]) & (row_index[None, :] <= row_index[:, None])
    local_scores = jnp.where(causal[None], local_scores, -jnp.inf)
    cache_rows = recv_pages.reshape(req_count, heads_local, 2, CAP * page_rows, HD)
    cache_rows = cache_rows.transpose(2, 1, 0, 3, 4).reshape(
        2, heads_local, slot_count * page_rows, HD
    )
    key_tags = jnp.repeat(slot_tags, page_rows)
    cached = masked_scores(query_rot, cache_rows[0], segment, key_tags, score_scale)
    row_max = jnp.maximum(jnp.max(local_scores, axis=2), jnp.max(cached, axis=2))
    local_exp = jnp.exp(local_scores - row_max[..., None])
    cached_exp = jnp.exp(cached - row_max[..., None])
    denominator = jnp.sum(local_exp, axis=2) + jnp.sum(cached_exp, axis=2)
    local_weights = (local_exp / denominator[..., None]).astype(jnp.bfloat16)
    cached_weights = (cached_exp / denominator[..., None]).astype(jnp.bfloat16)
    attention = jnp.einsum(
        "hqk,khd->qhd", local_weights, value_heads, preferred_element_type=jnp.float32
    )
    attention = attention + jnp.einsum(
        "hqk,hkd->qhd", cached_weights, cache_rows[1], preferred_element_type=jnp.float32
    )
    attn_flat = attention.astype(jnp.bfloat16).reshape(tok_count, heads_local * HD)
    return project(attn_flat, hidden, gathered, width)


def solution(mesh):
    return jax.shard_map(
        body,
        mesh=mesh,
        in_specs=(
            P("req", "tp"),
            P("req", "tp"),
            P("req", "tp"),
            P("req", "tp"),
            P("req", None, "tp", None),
            P("req", None),
            P("req"),
            P("req", None),
            P(("tp", "req"), None),
            P(("tp", "req"), None),
        ),
        out_specs=P("req", "tp"),
        check_vma=False,
    )
```

```python
import functools
import math

import jax
import jax.numpy as jnp
from jax import lax
from jax.experimental import pallas as pl
from jax.experimental.pallas import tpu as pltpu
from jax.sharding import PartitionSpec as P

HD = 128
ROT = 32
SEG_DEV = 4
CAP = 2
NX = 4
MESH = pl.DeviceIdType.MESH


def exchange_kernel(count, w_ref, p_ref, h_ref, pages_ref, tags_ref, g_ref, ha_ref, rp_ref, rt_ref,
                    via_ref, vt_ref, send, zr, zl, xp, xm, relay, psend, precv, tsend, trecv, wsend, wrecv,
                    hsend, hrecv, vsend, vrecv, vtsend, vtrecv):
    me = lax.axis_index("req")
    tp = lax.axis_index("tp")
    groups = ha_ref.shape[0]
    nz = count // NX
    half_z = nz // 2
    x = me // nz
    z = me % nz
    rows, proj = w_ref.shape[0], p_ref.shape[2]
    width = w_ref.shape[1] // groups

    def at(dx, dz):
        return ((x + dx + NX) % NX) * nz + (z + dz + nz) % nz

    def shard(owner, first=0, size=groups):
        return g_ref.at[pl.ds(first, size), pl.ds(pl.multiple_of(owner * rows, rows), rows), :]

    def shards(number):
        return g_ref.at[:, pl.ds(0, number * rows), :]

    barrier = pltpu.get_barrier_semaphore()

    def greet_tp(i, carry):
        pl.semaphore_signal(
            barrier, inc=1, device_id={"tp": (tp + i) % groups}, device_id_type=MESH
        )
        return carry

    def greet(i, carry):
        pl.semaphore_signal(
            barrier, inc=1, device_id={"req": (me + i) % count}, device_id_type=MESH
        )
        return carry

    lax.fori_loop(1, groups, greet_tp, 0)
    lax.fori_loop(1, count, greet, 0)
    pl.semaphore_wait(barrier, count + groups - 2)

    def push(ref, recv_sem, to):
        pltpu.make_async_remote_copy(
            src_ref=ref, dst_ref=ref, send_sem=send.at[0], recv_sem=recv_sem,
            device_id={"req": to}, device_id_type=MESH,
        ).start()

    def arrived(ref, sem):
        pltpu.make_async_copy(ref, ref, sem).wait()

    own = pl.ds(pl.multiple_of(me * rows, rows), rows)
    down_slot = g_ref.at[tp, own, pl.ds(0, width)]
    proj_slot = g_ref.at[tp, own, pl.ds(width, proj)]

    def down_of(g):
        return w_ref.at[:, pl.ds(pl.multiple_of(g * width, width), width)]

    def columns_to(i, carry):
        to = (tp + i) % groups
        for src, dst in ((down_of(to), down_slot), (p_ref.at[to], proj_slot)):
            pltpu.make_async_remote_copy(
                src_ref=src, dst_ref=dst, send_sem=wsend.at[0], recv_sem=wrecv.at[0],
                device_id={"tp": to}, device_id_type=MESH,
            ).start()
        return carry

    def hidden_to(i, carry):
        pltpu.make_async_remote_copy(
            src_ref=h_ref, dst_ref=ha_ref.at[tp], send_sem=hsend.at[0], recv_sem=hrecv.at[0],
            device_id={"tp": (tp + i) % groups}, device_id_type=MESH,
        ).start()
        return carry

    def to_req(src, dst, send_sem, recv_sem, to):
        pltpu.make_async_remote_copy(
            src_ref=src, dst_ref=dst, send_sem=send_sem, recv_sem=recv_sem,
            device_id={"req": to}, device_id_type=MESH,
        ).start()

    def pages(dz, first, stop=NX):
        def one(dx, carry):
            to = at(dx, dz)
            to_req(pages_ref.at[to], rp_ref.at[me], psend.at[0], precv.at[0], to)
            to_req(tags_ref.at[to], rt_ref.at[me], tsend.at[0], trecv.at[0], to)
            return carry

        lax.fori_loop(first, stop, one, 0)

    hops = half_z // 2
    direct = NX // 2

    def by_stop(dx, carry):
        to = at(dx, -half_z)
        to_req(pages_ref.at[to], via_ref.at[dx - direct], psend.at[0], vrecv.at[0], at(0, -hops))
        to_req(tags_ref.at[to], vt_ref.at[dx - direct], tsend.at[0], vtrecv.at[0], at(0, -hops))
        return carry

    def onward(dx, carry):
        to, source = at(dx, -hops), at(0, hops)
        to_req(via_ref.at[dx - direct], rp_ref.at[source], vsend.at[0], precv.at[0], to)
        to_req(vt_ref.at[dx - direct], rt_ref.at[source], vtsend.at[0], trecv.at[0], to)
        return carry

    lax.fori_loop(1, groups, columns_to, 0)
    pltpu.make_async_copy(down_of(tp), down_slot, wrecv.at[0]).start()
    pltpu.make_async_copy(p_ref.at[tp], proj_slot, wrecv.at[0]).start()
    pages(half_z, 0, direct)
    lax.fori_loop(direct, NX, by_stop, 0)
    lax.fori_loop(1, groups, hidden_to, 0)
    pltpu.make_async_copy(h_ref, ha_ref.at[tp], hrecv.at[0]).start()
    pltpu.make_async_copy(pages_ref.at[me], rp_ref.at[me], precv.at[0]).start()
    pltpu.make_async_copy(tags_ref.at[me], rt_ref.at[me], trecv.at[0]).start()

    right, left = at(0, 1), at(0, -1)
    plus, minus = at(1, 0), at(-1, 0)

    def relays(dz, slot):
        below, above = at(-1, dz), at(1, dz)
        arrived(shard(below), xp.at[slot])
        push(shard(below, 0, groups // 2), relay.at[0], plus)
        arrived(shard(above), xm.at[slot])
        push(shard(above, groups // 2, groups // 2), relay.at[0], minus)

    mine = shard(me)
    arrived(mine, wrecv.at[0])
    push(mine, zr.at[0], right)
    push(mine, zl.at[0], left)
    push(mine, xp.at[0], plus)
    push(mine, xm.at[0], minus)
    for s in range(1, half_z + 1):
        below = shard(at(0, -s))
        arrived(below, zr.at[s - 1])
        if s < half_z:
            push(below, zr.at[s], right)
        push(below, xp.at[2 * s - 1], plus)
        push(below, xm.at[2 * s - 1], minus)
        if s < half_z:
            above = shard(at(0, s))
            arrived(above, zl.at[s - 1])
            if s < half_z - 1:
                push(above, zl.at[s], left)
            push(above, xp.at[2 * s], plus)
            push(above, xm.at[2 * s], minus)
        far = half_z - s
        pages(far, 0 if far else 1)
        if far:
            pages(-far, 0)
        if s == 2:
            arrived(via_ref, vrecv.at[0])
            arrived(vt_ref, vtrecv.at[0])
            lax.fori_loop(direct, NX, onward, 0)
        if s == 1:
            relays(0, 0)
        else:
            relays(-(s - 1), 2 * s - 3)
            relays(s - 1, 2 * s - 2)
    relays(-half_z, 2 * half_z - 1)
    arrived(shards(nz), relay.at[0])
    arrived(shards(count - 1), send.at[0])
    arrived(rp_ref, precv.at[0])
    arrived(rt_ref, trecv.at[0])
    arrived(ha_ref, hrecv.at[0])
    arrived(rp_ref.at[pl.ds(0, count - 1)], psend.at[0])
    arrived(rt_ref.at[pl.ds(0, count - 1)], tsend.at[0])
    arrived(via_ref, vsend.at[0])
    arrived(vt_ref, vtsend.at[0])
    arrived(ha_ref.at[pl.ds(0, groups - 1)], hsend.at[0])
    arrived(g_ref.at[pl.ds(0, groups - 1), pl.ds(0, rows), :], wsend.at[0])


def exchange(down, proj, hidden, send_pages, send_tags):
    count = send_pages.shape[0]
    groups = proj.shape[0]
    half_z = count // NX // 2
    any_space = pl.BlockSpec(memory_space=pl.ANY)
    dma = pltpu.SemaphoreType.DMA
    rows = down.shape[0]
    width = down.shape[1] // groups + proj.shape[2]
    return pl.pallas_call(
        functools.partial(exchange_kernel, count),
        out_shape=(
            jax.ShapeDtypeStruct((groups, count * rows, width), down.dtype),
            jax.ShapeDtypeStruct((groups,) + hidden.shape, hidden.dtype),
            jax.ShapeDtypeStruct(send_pages.shape, send_pages.dtype),
            jax.ShapeDtypeStruct(send_tags.shape, send_tags.dtype),
        ),
        in_specs=[pl.BlockSpec(memory_space=pltpu.VMEM)] * 5,
        out_specs=(any_space,) * 4,
        scratch_shapes=[
            pltpu.VMEM((NX - NX // 2,) + send_pages.shape[1:], send_pages.dtype),
            pltpu.VMEM((NX - NX // 2,) + send_tags.shape[1:], send_tags.dtype),
            dma((1,)), dma((half_z,)), dma((half_z,)), dma((2 * half_z,)), dma((2 * half_z,)),
        ] + [dma((1,))] * 13,
        compiler_params=pltpu.CompilerParams(collective_id=0, has_side_effects=True),
        name="exchange",
    )(down, proj, hidden, send_pages, send_tags)


def project_kernel(groups, part_ref, h_ref, g_ref, out_ref,
                   all_ref, hid, wts, total, wide, flat, send, recv, hsem, gsem):
    me = lax.axis_index("tp")
    width = out_ref.shape[1]
    lanes = g_ref.shape[2] - width
    depth = part_ref.shape[1]

    def load(g, carry):
        pltpu.make_async_copy(h_ref.at[g], hid.at[g], hsem.at[g]).start()
        pltpu.make_async_copy(g_ref.at[g], wts.at[g], gsem.at[g]).start()
        return carry

    barrier = pltpu.get_barrier_semaphore()
    for i in range(1, groups):
        pl.semaphore_signal(
            barrier, inc=1, device_id={"tp": (me + i) % groups}, device_id_type=MESH
        )
    lax.fori_loop(0, groups, load, 0)
    pl.semaphore_wait(barrier, groups - 1)
    for i in range(1, groups):
        pltpu.make_async_remote_copy(
            src_ref=part_ref, dst_ref=all_ref.at[me], send_sem=send.at[0], recv_sem=recv.at[0],
            device_id={"tp": (me + i) % groups}, device_id_type=MESH,
        ).start()
    pltpu.make_async_copy(part_ref, all_ref.at[me], recv.at[0]).start()
    total[...] = jnp.zeros_like(total)

    def local_term(g, carry):
        pltpu.make_async_copy(h_ref.at[g], hid.at[g], hsem.at[g]).wait()
        pltpu.make_async_copy(g_ref.at[g], wts.at[g], gsem.at[g]).wait()
        total[...] += jnp.dot(hid[g], wts[g, :, :width], preferred_element_type=jnp.float32)
        wide[...] = wts[g, :, width:].astype(jnp.float32)
        for c in range(width // lanes):
            flat[g, :, c * lanes:(c + 1) * lanes] = wide[
                pl.ds(c, depth, stride=width // lanes), :
            ].astype(flat.dtype)
        return carry

    lax.fori_loop(0, groups, local_term, 0)
    pltpu.make_async_copy(all_ref, all_ref, recv.at[0]).wait()

    def spread_term(g, carry):
        total[...] += jnp.dot(all_ref[g], flat[g], preferred_element_type=jnp.float32)
        return carry

    lax.fori_loop(0, groups, spread_term, 0)
    out_ref[...] = total[...].astype(out_ref.dtype)
    rest = all_ref.at[pl.ds(0, groups - 1)]
    pltpu.make_async_copy(rest, rest, send.at[0]).wait()


def project(part, hidden, gathered, width):
    groups, units = gathered.shape[:2]
    tokens, depth = part.shape
    lanes = gathered.shape[2] - width
    vmem = pl.BlockSpec(memory_space=pltpu.VMEM)
    any_space = pl.BlockSpec(memory_space=pl.ANY)
    dma = pltpu.SemaphoreType.DMA
    return pl.pallas_call(
        functools.partial(project_kernel, groups),
        out_shape=jax.ShapeDtypeStruct((tokens, width), part.dtype),
        in_specs=[vmem, any_space, any_space],
        out_specs=vmem,
        scratch_shapes=[
            pltpu.VMEM((groups,) + part.shape, part.dtype),
            pltpu.VMEM(hidden.shape, hidden.dtype),
            pltpu.VMEM(gathered.shape, gathered.dtype),
            pltpu.VMEM((tokens, width), jnp.float32),
            pltpu.VMEM((units, lanes), jnp.float32),
            pltpu.VMEM((groups, depth, width), part.dtype),
            dma((1,)), dma((1,)), dma((groups,)), dma((groups,)),
        ],
        compiler_params=pltpu.CompilerParams(collective_id=1, has_side_effects=True),
        name="project",
    )(part, hidden, gathered)


def rotate_heads(values, position, rot_dims):
    half_rot = rot_dims // 2
    frequency = 10000.0 ** (-2.0 * jnp.arange(half_rot, dtype=jnp.float32) / rot_dims)
    angles = position.astype(jnp.float32)[:, None] * frequency[None, :]
    cosine = jnp.cos(angles)[:, None, :]
    sine_part = jnp.sin(angles)[:, None, :]
    leading = values[..., :half_rot]
    trailing = values[..., half_rot:rot_dims]
    return jnp.concatenate(
        [
            leading * cosine - trailing * sine_part,
            trailing * cosine + leading * sine_part,
            values[..., rot_dims:],
        ],
        axis=-1,
    )


def masked_scores(query_rot, block_keys, segment, block_tags, score_scale):
    scores = (
        jnp.einsum("qhd,hkd->hqk", query_rot, block_keys, preferred_element_type=jnp.float32)
        * score_scale
    )
    return jnp.where((segment[:, None] == block_tags[None, :])[None], scores, -jnp.inf)


def body(
    query_new,
    key_new,
    value_new,
    mlp_hidden,
    cache_pages,
    page_dest,
    page_tag,
    seg_ids,
    attn_proj,
    mlp_down,
):
    req_count = lax.axis_size("req")
    tok_count = query_new.shape[0]
    heads_local = query_new.shape[1] // HD
    page_rows = cache_pages.shape[1]
    pages_local = cache_pages.shape[0]
    slot_count = req_count * CAP
    score_scale = 1.0 / math.sqrt(HD)
    destination = page_dest[:, 0]
    dest_match = (destination[:, None] == jnp.arange(req_count, dtype=jnp.int32)[None, :]).astype(
        jnp.int32
    )
    earlier = jnp.cumsum(dest_match, axis=0) - dest_match
    rank = jnp.sum(earlier * dest_match, axis=1)
    slot_of_page = destination * CAP + rank
    select = jnp.arange(slot_count, dtype=jnp.int32)[:, None] == slot_of_page[None, :]
    flat_pages = cache_pages.reshape(pages_local, page_rows * heads_local * 2 * HD)
    send_pages = jnp.dot(
        select.astype(jnp.bfloat16), flat_pages, preferred_element_type=jnp.float32
    ).astype(jnp.bfloat16)
    blocks = 2 * heads_local
    send_pages = (
        send_pages.reshape(req_count, CAP * page_rows, blocks, HD).transpose(0, 2, 1, 3)
    )
    send_tags = (
        jnp.sum(jnp.where(select, page_tag[None, :] + 1, 0), axis=1) - 1
    ).reshape(req_count, 1, CAP)
    send_tags = jnp.pad(send_tags, ((0, 0), (0, 0), (0, HD - CAP)))
    groups = lax.axis_size("tp")
    shard_rows = mlp_down.shape[0]
    proj_rows = attn_proj.shape[0]
    width = mlp_down.shape[1] // groups
    proj = attn_proj.reshape(proj_rows, groups, shard_rows // proj_rows, -1)
    proj = proj.transpose(1, 0, 2, 3).reshape(groups, shard_rows, -1)
    gathered, hidden, recv_pages, recv_tags = exchange(
        mlp_down, proj, mlp_hidden, send_pages, send_tags
    )
    slot_tags = recv_tags[:, 0, :CAP].reshape(slot_count)
    segment = seg_ids[0]
    seg_range = jnp.arange(SEG_DEV, dtype=jnp.int32)
    seg_first = jnp.sum((segment[:, None] < seg_range[None, :]).astype(jnp.int32), axis=0)
    prefix = page_rows * jnp.sum(
        (slot_tags[:, None] == seg_range[None, :]).astype(jnp.int32), axis=0
    )
    seg_match = segment[:, None] == seg_range[None, :]
    offset = jnp.sum(jnp.where(seg_match, prefix[None, :] - seg_first[None, :], 0), axis=1)
    row_index = jnp.arange(tok_count, dtype=jnp.int32)
    position = row_index + offset
    query_rot = rotate_heads(
        query_new.reshape(tok_count, heads_local, HD).astype(jnp.float32), position, ROT
    ).astype(jnp.bfloat16)
    key_rot = rotate_heads(
        key_new.reshape(tok_count, heads_local, HD).astype(jnp.float32), position, ROT
    ).astype(jnp.bfloat16)
    value_heads = value_new.reshape(tok_count, heads_local, HD)
    local_scores = (
        jnp.einsum("qhd,khd->hqk", query_rot, key_rot, preferred_element_type=jnp.float32)
        * score_scale
    )
    causal = (segment[:, None] == segment[None, :]) & (row_index[None, :] <= row_index[:, None])
    local_scores = jnp.where(causal[None], local_scores, -jnp.inf)
    cache_rows = recv_pages.reshape(req_count, heads_local, 2, CAP * page_rows, HD)
    cache_rows = cache_rows.transpose(2, 1, 0, 3, 4).reshape(
        2, heads_local, slot_count * page_rows, HD
    )
    key_tags = jnp.repeat(slot_tags, page_rows)
    cached = masked_scores(query_rot, cache_rows[0], segment, key_tags, score_scale)
    row_max = jnp.maximum(jnp.max(local_scores, axis=2), jnp.max(cached, axis=2))
    local_exp = jnp.exp(local_scores - row_max[..., None])
    cached_exp = jnp.exp(cached - row_max[..., None])
    denominator = jnp.sum(local_exp, axis=2) + jnp.sum(cached_exp, axis=2)
    local_weights = (local_exp / denominator[..., None]).astype(jnp.bfloat16)
    cached_weights = (cached_exp / denominator[..., None]).astype(jnp.bfloat16)
    attention = jnp.einsum(
        "hqk,khd->qhd", local_weights, value_heads, preferred_element_type=jnp.float32
    )
    attention = attention + jnp.einsum(
        "hqk,hkd->qhd", cached_weights, cache_rows[1], preferred_element_type=jnp.float32
    )
    attn_flat = attention.astype(jnp.bfloat16).reshape(tok_count, heads_local * HD)
    return project(attn_flat, hidden, gathered, width)


def solution(mesh):
    return jax.shard_map(
        body,
        mesh=mesh,
        in_specs=(
            P("req", "tp"),
            P("req", "tp"),
            P("req", "tp"),
            P("req", "tp"),
            P("req", None, "tp", None),
            P("req", None),
            P("req"),
            P("req", None),
            P(("tp", "req"), None),
            P(("tp", "req"), None),
        ),
        out_specs=P("req", "tp"),
        check_vma=False,
    )
```
